32 devices in a mesh: groups: 2 (over y), shard: 4 (over z), dp: 2 (over x), tok: 2 (over core).
Axes of the slice: x: 2, y: 2, z: 4, core: 2. Of those that a mesh axis runs over, the one named last changes fastest.
Arguments:
- tokens: bfloat16 [2048, 4096], P(('groups', 'dp', 'tok'), 'shard'), parts along dimension 0, may hold values from -6 to 6
- gate_blocks: bfloat16 [8, 16, 128, 128], P('shard'), may hold values from -0.125 to 0.125
- up_blocks: bfloat16 [8, 16, 128, 128], P('shard'), may hold values from -0.125 to 0.125
- down_blocks: bfloat16 [8, 16, 128, 128], P('shard'), may hold values from -0.25 to 0.25
- gate_rows: int32 [8, 16], P('shard'), may hold values from 0 to 31, as said below
- up_rows: int32 [8, 16], P('shard'), may hold values from 0 to 31, as said below
- down_rows: int32 [8, 16], replicated, may hold values from 0 to 31, as said below
- cotangent: bfloat16 [2048, 4096], P(('groups', 'dp', 'tok'), 'shard'), parts along dimension 0, may hold values from -6 to 6
Outputs:
- mixed: bfloat16 [2048, 4096], P(('groups', 'dp', 'tok'), 'shard'), parts along dimension 0
- tokens_grad: bfloat16 [2048, 4096], P(('groups', 'dp', 'tok'), 'shard'), parts along dimension 0
- gate_grad: bfloat16 [16, 16, 128, 128], P(('groups', 'shard'), ('dp', 'tok')), parts along dimension 0
- up_grad: bfloat16 [16, 16, 128, 128], P(('groups', 'shard'), ('dp', 'tok')), parts along dimension 0
- down_grad: bfloat16 [16, 16, 128, 128], P(('groups', 'shard'), ('dp', 'tok')), parts along dimension 0
The draws below stay inside these ranges and needn't reach their ends.
There are 2 independent parts, one for each index of `groups`. The reference program is written for one: setup_inputs(seed, part) draws one part's arguments, and reference() takes and returns one part's arrays. A program takes and returns all parts, laid end to end along the dimension named above; an argument that names none is the same for every part. Nothing has to cross between parts.
Inputs may be any that keep to these rules, and one draw needn't show every extreme that they name: `gate_rows`: in every row c of the list and for every o, the entries o * 4 to (o + 1) * 4 - 1 are distinct blocks among o * 2 * 4 to (o + 1) * 2 * 4 - 1, in ascending order. `up_rows`: as for gate_rows, drawn independently. `down_rows`: as for gate_rows, drawn independently.
All inputs are finite; a program needn't handle non-finite values.
Results may differ from the reference program's by a relative error of at most 0.018.
Values may be sent and summed in bfloat16 or wider, within the bound.
No kernel may reach another device: no remote copies, remote signals or barrier semaphores. Data moves between devices by JAX's collectives and lax.ppermute only.
A program may use at most 64 MiB of HBM per device.

```python
import jax
import jax.numpy as jnp
from jax import lax

D = 4096
BLOCK = 128
TOKENS = 1024
COLS = 8
FF = 1024
NZC = 16
HALF = 4
N_DP = 2
N_TOK = 2


def pick_rows(key):
    group = 2 * HALF
    owners = D // BLOCK // group
    scores = jax.random.randint(key, (COLS, owners, group), 0, 1 << 20)
    scores = scores * group + jnp.arange(group, dtype=jnp.int32)
    order = jnp.argsort(scores, axis=-1).astype(jnp.int32)
    chosen = jnp.sort(order[:, :, :HALF], axis=-1)
    offsets = (jnp.arange(owners, dtype=jnp.int32) * group)[None, :, None]
    return (chosen + offsets).reshape(COLS, owners * HALF).astype(jnp.int32)


def draw_gate_rows(key, part):
    return pick_rows(jax.random.fold_in(key, 11))


def draw_up_rows(key, part):
    return pick_rows(jax.random.fold_in(key, 23))


def draw_down_rows(key, part):
    return pick_rows(jax.random.fold_in(key, 37))


def shard_levels(own_key, extent, shards, low, top_value):
    factor_of, own = 1.0, jax.random.fold_in(own_key, 6)
    for dim, blocks in shards:
        steps = jnp.exp(jax.random.uniform(jax.random.fold_in(own, dim), (blocks,), jnp.float32, low / len(shards), top_value / len(shards)))
        factor_of = factor_of * jnp.repeat(steps, extent[dim] // blocks).reshape([-1 if axis == dim else 1 for axis in range(len(extent))])
    return factor_of


def gaussian(stream_key, dims, deviation, bound, pieces=(), held_as=jnp.bfloat16):
    level = shard_levels(stream_key, dims, pieces, -0.22, 0.18) if pieces else 1.0
    drawn = jax.random.normal(stream_key, dims, jnp.float32) * deviation * level
    return jnp.minimum(jnp.maximum(drawn, -bound), bound).astype(held_as)


def setup_inputs(seed: int = 0, part: int = 0) -> dict:
    keys = jax.random.split(jax.random.key(seed), 9)
    part_keys = jax.random.split(jax.random.fold_in(keys[8], part), 9)
    tokens = gaussian(part_keys[0], (TOKENS, D), 1.0, 6.0, ((0, 4), (1, 4)))
    gate_blocks = gaussian(keys[1], (COLS, NZC, BLOCK, BLOCK), (D // 2) ** -0.5, 0.125, ((0, 4),))
    up_blocks = gaussian(keys[2], (COLS, NZC, BLOCK, BLOCK), (D // 2) ** -0.5, 0.125, ((0, 4),))
    down_blocks = gaussian(keys[3], (COLS, NZC, BLOCK, BLOCK), (FF // 2) ** -0.5, 0.25, ((0, 4),))
    gate_rows = draw_gate_rows(jax.random.fold_in(keys[8], 71), part)
    up_rows = draw_up_rows(jax.random.fold_in(keys[8], 71), part)
    down_rows = draw_down_rows(jax.random.fold_in(keys[8], 71), part)
    cotangent = gaussian(part_keys[7], (TOKENS, D), 1.0, 6.0, ((0, 4), (1, 4)))
    return dict(tokens=tokens, gate_blocks=gate_blocks, up_blocks=up_blocks, down_blocks=down_blocks, gate_rows=gate_rows, up_rows=up_rows, down_rows=down_rows, cotangent=cotangent)


def block_partials(left, right, form):
    replicas = N_DP * N_TOK
    left_r = left.reshape((replicas, left.shape[0] // replicas) + left.shape[1:])
    right_r = right.reshape((replicas, right.shape[0] // replicas) + right.shape[1:])
    partial_sums = jnp.einsum(form, left_r, right_r)
    rounded = lax.optimization_barrier(partial_sums.astype(jnp.bfloat16))
    return jnp.sum(rounded.astype(jnp.float32), axis=0).astype(jnp.bfloat16)


def reference(tokens, gate_blocks, up_blocks, down_blocks, gate_rows, up_rows, down_rows, cotangent):
    token_count = tokens.shape[0]
    width = tokens.shape[1]
    block_size = gate_blocks.shape[2]
    row_blocks = width // block_size
    tokens3 = tokens.reshape(token_count, row_blocks, block_size).astype(jnp.float32)
    cotangent3 = cotangent.reshape(token_count, row_blocks, block_size).astype(jnp.float32)

    def one_column(carry, column):
        out_sum, grad_sum = carry
        gate_weight, up_weight, down_weight, gate_list, up_list, down_list = column
        gate_weight = gate_weight.astype(jnp.float32)
        up_weight = up_weight.astype(jnp.float32)
        down_weight = down_weight.astype(jnp.float32)
        gate_in = jnp.take(tokens3, gate_list, axis=1)
        up_in = jnp.take(tokens3, up_list, axis=1)
        gate = jnp.einsum("nkb,kbc->nc", gate_in, gate_weight)
        up = jnp.einsum("nkb,kbc->nc", up_in, up_weight)
        hidden = (jax.nn.silu(gate) * up).astype(jnp.bfloat16)
        hidden_wide = hidden.astype(jnp.float32)
        out_blocks = jnp.einsum("nb,kbo->nko", hidden_wide, down_weight)
        out_term = jnp.zeros_like(out_sum).at[:, down_list].set(out_blocks)
        out_term = lax.optimization_barrier(out_term.astype(jnp.bfloat16))
        out_sum = out_sum + out_term.astype(jnp.float32)
        cot_in = jnp.take(cotangent3, down_list, axis=1)
        hidden_grad = jnp.einsum("nko,kbo->nb", cot_in, down_weight)
        sigmoid_gate = jax.nn.sigmoid(gate)
        gate_act = (hidden_grad * up * sigmoid_gate * (1.0 + gate * (1.0 - sigmoid_gate))).astype(jnp.bfloat16)
        up_act = (hidden_grad * jax.nn.silu(gate)).astype(jnp.bfloat16)
        gate_act_wide = gate_act.astype(jnp.float32)
        up_act_wide = up_act.astype(jnp.float32)
        back_gate = jnp.einsum("nc,kbc->nkb", gate_act_wide, gate_weight)
        back_up = jnp.einsum("nc,kbc->nkb", up_act_wide, up_weight)
        in_term = jnp.zeros_like(grad_sum).at[:, gate_list].add(back_gate).at[:, up_list].add(back_up)
        in_term = lax.optimization_barrier(in_term.astype(jnp.bfloat16))
        grad_sum = grad_sum + in_term.astype(jnp.float32)
        gate_grad = block_partials(gate_in, gate_act_wide, "rtkb,rtc->rkbc")
        up_grad = block_partials(up_in, up_act_wide, "rtkb,rtc->rkbc")
        down_grad = block_partials(hidden_wide, cot_in, "rtb,rtko->rkbo")
        return (out_sum, grad_sum), (gate_grad, up_grad, down_grad)

    start = jnp.zeros((token_count, row_blocks, block_size), jnp.float32)
    (out_sum, grad_sum), grads = lax.scan(one_column, (start, start), (gate_blocks, up_blocks, down_blocks, gate_rows, up_rows, down_rows))
    mixed = out_sum.reshape(token_count, width).astype(jnp.bfloat16)
    tokens_grad = grad_sum.reshape(token_count, width).astype(jnp.bfloat16)
    return (mixed, tokens_grad, grads[0], grads[1], grads[2])
```

```python
import functools

import jax
import jax.numpy as jnp
from jax import lax
from jax.experimental import pallas as pl
from jax.experimental.pallas import tpu as pltpu
from jax.sharding import PartitionSpec as P

BF = jnp.bfloat16
F32 = jnp.float32
PLANE = ("shard", "dp", "tok")


def xor_perm(count, step):
    return [(i, i ^ step) for i in range(count)]


def weight_perm(shards, n_dp, n_tok):
    pairs = []
    for z in range(shards):
        for x in range(n_dp):
            for c in range(n_tok):
                q = c * n_dp + x
                pairs.append((q * n_dp * n_tok + weight_source(shards, n_dp, n_tok, q, z), (z * n_dp + x) * n_tok + c))
    return pairs


def weight_source(shards, n_dp, n_tok, q, z):
    if (shards, n_dp, n_tok) == (4, 2, 2):
        x = q % 2
        far = (q < 2) != (z < 2)
        return (x if far else 1 - x) * 2 + z % 2
    return z


def weight_target(shards, n_dp, n_tok):
    table = [0] * (shards * n_dp * n_tok)
    for q in range(shards):
        for z in range(shards):
            table[q * n_dp * n_tok + weight_source(shards, n_dp, n_tok, q, z)] = z
    return table


def grad_perm(shards, n_dp, n_tok):
    return [
        ((z * n_dp + x) * n_tok + c, (c * n_dp + x) * n_dp * n_tok + z)
        for z in range(shards)
        for x in range(n_dp)
        for c in range(n_tok)
    ]


def vmem(count):
    return [pl.BlockSpec(memory_space=pltpu.VMEM)] * count


def smem(count):
    return [pl.BlockSpec(memory_space=pltpu.SMEM)] * count


def call(kernel, scalars, arrays, outs, scratch, flops, name):
    moved = sum(a.size * a.dtype.itemsize for a in arrays)
    moved += sum(o.size * o.dtype.itemsize for o in outs)
    return pl.pallas_call(
        kernel,
        out_shape=outs,
        in_specs=smem(len(scalars)) + vmem(len(arrays)),
        out_specs=vmem(len(outs)),
        scratch_shapes=scratch,
        cost_estimate=pl.CostEstimate(flops=flops, bytes_accessed=moved, transcendentals=0),
        name=name,
    )(*scalars, *arrays)


def aligned(value, size):
    return pl.multiple_of(value * size, size)


def scatter_rows(dense, blocks, rows):
    columns, per_owner, size, _ = blocks.shape
    dense[...] = jnp.zeros_like(dense)
    for c in range(columns):
        for k in range(per_owner):
            dense[pl.ds(aligned(rows[c, k], size), size), c * size : (c + 1) * size] = blocks[c, k]


def scatter_cols(dense, blocks, rows):
    columns, per_owner, size, _ = blocks.shape
    dense[...] = jnp.zeros_like(dense)
    for c in range(columns):
        for k in range(per_owner):
            dense[c * size : (c + 1) * size, pl.ds(aligned(rows[c, k], size), size)] = blocks[c, k]


def split_rows(total, r, slot, outs, z):
    rows = outs[0].shape[2]
    for d, out in enumerate(outs):
        out[slot, r] = total[r, pl.ds(aligned(z ^ d, rows), rows), :].astype(out.dtype)


def gate_up_kernel(shards, nj, z_ref, gate_rows, up_rows, *refs):
    xs = refs[:nj]
    gate_blocks, up_blocks = refs[nj : nj + 2]
    outs = refs[nj + 2 : nj + 2 + shards]
    gate_dense, up_dense = refs[nj + 2 + shards : nj + 4 + shards]
    gate_total, up_total = refs[nj + 4 + shards :]
    z = z_ref[0]
    scatter_rows(gate_dense, gate_blocks, gate_rows)
    scatter_rows(up_dense, up_blocks, up_rows)
    for r in range(nj):
        x = xs[r][...]
        gate_total[r] = jnp.dot(x, gate_dense[...], preferred_element_type=F32)
        split_rows(gate_total, r, 0, outs, z)
        up_total[r] = jnp.dot(x, up_dense[...], preferred_element_type=F32)
        split_rows(up_total, r, 1, outs, z)


def hidden_grad_kernel(shards, nj, z_ref, down_rows, *refs):
    cots = refs[:nj]
    down_blocks = refs[nj]
    outs = refs[nj + 1 : nj + 1 + shards]
    down_dense = refs[nj + 1 + shards]
    total = refs[nj + 2 + shards]
    z = z_ref[0]
    scatter_cols(down_dense, down_blocks, down_rows)
    for r in range(nj):
        total[r] = lax.dot_general(
            cots[r][...], down_dense[...], (((1,), (1,)), ((), ())), preferred_element_type=F32
        )
        split_rows(total, r, 0, outs, z)


def hidden_kernel(*refs):
    parts, (sums, hidden) = refs[:-2], refs[-2:]
    gate = sum(part[0].astype(F32) for part in parts)
    up = sum(part[1].astype(F32) for part in parts)
    sums[0] = gate
    sums[1] = up
    hidden[...] = (gate * jax.nn.sigmoid(gate) * up).astype(BF)


def act_grad_kernel(sums, *refs):
    parts, (gate_act, up_act) = refs[:-2], refs[-2:]
    hidden_grad = sum(part[0].astype(F32) for part in parts)
    gate, up = sums[0], sums[1]
    s = jax.nn.sigmoid(gate)
    gate_act[...] = (hidden_grad * up * s * (1.0 + gate * (1.0 - s))).astype(BF)
    up_act[...] = (hidden_grad * (gate * s)).astype(BF)


def join_rows(joined, parts, z):
    rows = parts[0].shape[1]
    for r in range(joined.shape[0]):
        for d, part in enumerate(parts):
            joined[r, pl.ds(aligned(z ^ d, rows), rows), :] = part[r]


def weight_grad(acc, left, rights):
    for r, right in enumerate(rights):
        term = lax.dot_general(left[r], right[...], (((0,), (0,)), ((), ())), preferred_element_type=F32)
        if r == 0:
            acc[...] = term
        else:
            acc[...] += term


def pick_blocks(out, acc, rows, transposed):
    columns, per_owner, size, _ = out.shape
    for c in range(columns):
        for k in range(per_owner):
            block = acc[c * size : (c + 1) * size, pl.ds(aligned(rows[c, k], size), size)]
            out[c, k] = (block.T if transposed else block).astype(BF)


def put_plane(keep, send, r, n_tok, value):
    dx, dc = divmod(r, n_tok)
    if dc == 0:
        keep[dx] = value
    else:
        send[dx][dc - 1] = value.astype(BF)


def mixed_kernel(shards, nj, n_tok, z_ref, down_rows, *refs):
    hiddens = refs[:shards]
    dense = refs[shards]
    cots = refs[shards + 1 : shards + 1 + nj]
    rest = refs[shards + 1 + nj :]
    keep, send = rest[0], rest[1 : 1 + nj // n_tok]
    grad, joined, acc = rest[1 + nj // n_tok :]
    join_rows(joined, hiddens, z_ref[0])
    for r in reversed(range(nj)):
        put_plane(keep, send, r, n_tok, jnp.dot(joined[r], dense[...], preferred_element_type=F32))
    weight_grad(acc, joined, cots)
    pick_blocks(grad, acc, down_rows, False)


def gate_grad_kernel(shards, nj, z_ref, rows, *refs):
    acts = refs[:shards]
    xs = refs[shards : shards + nj]
    grad, joined, acc = refs[shards + nj :]
    join_rows(joined, acts, z_ref[0])
    weight_grad(acc, joined, xs)
    pick_blocks(grad, acc, rows, True)


def tokens_grad_kernel(shards, nj, n_tok, z_ref, rows, *refs):
    acts = refs[:shards]
    joined_gate, gate_dense, up_dense = refs[shards : shards + 3]
    xs = refs[shards + 3 : shards + 3 + nj]
    rest = refs[shards + 3 + nj :]
    keep, send = rest[0], rest[1 : 1 + nj // n_tok]
    grad, joined, acc = rest[1 + nj // n_tok :]
    join_rows(joined, acts, z_ref[0])
    contract = (((1,), (1,)), ((), ()))
    for r in reversed(range(nj)):
        value = lax.dot_general(joined_gate[r], gate_dense[...], contract, preferred_element_type=F32)
        value += lax.dot_general(joined[r], up_dense[...], contract, preferred_element_type=F32)
        put_plane(keep, send, r, n_tok, value)
    weight_grad(acc, joined, xs)
    pick_blocks(grad, acc, rows, True)


def shape(dims, dtype):
    return jax.ShapeDtypeStruct(dims, dtype)


def body(n_dp, n_tok, shards, tokens, gate_blocks, up_blocks, down_blocks, gate_rows, up_rows, down_rows, cotangent):
    nj = n_dp * n_tok
    z = lax.axis_index("shard")
    x_index, c_index = lax.axis_index("dp"), lax.axis_index("tok")
    q = c_index * n_dp + x_index
    count, width = tokens.shape
    columns, nonzero, size, _ = gate_blocks.shape
    per_owner = nonzero // shards
    owned = width // size
    hidden_width = columns * size
    part = count // shards
    z_arr = z.astype(jnp.int32).reshape(1)

    w_perm = weight_perm(shards, n_dp, n_tok)
    table = jnp.array(weight_target(shards, n_dp, n_tok), jnp.int32)
    owner = table[z * nj + x_index * n_tok + c_index]
    take = lambda a: lax.dynamic_slice_in_dim(a, owner * per_owner, per_owner, 1)
    lists = jnp.stack([take(gate_rows), take(up_rows)]) - owner * owned
    lists = lax.ppermute(lists, PLANE, w_perm)
    my_gate_blocks = lax.ppermute(take(gate_blocks), PLANE, w_perm)
    my_up_blocks = lax.ppermute(take(up_blocks), PLANE, w_perm)
    my_down_blocks = lax.ppermute(take(down_blocks), PLANE, w_perm)
    g_rows, u_rows = lists[0], lists[1]
    d_rows = lax.dynamic_slice(down_rows, (q * columns, z * per_owner), (columns, per_owner)) - z * owned

    def gather_plane(own):
        got = []
        for dx in range(n_dp):
            base = own if dx == 0 else lax.ppermute(own, "dp", xor_perm(n_dp, dx))
            got.append(base)
            got += [lax.ppermute(base, "tok", xor_perm(n_tok, dc)) for dc in range(1, n_tok)]
        return got

    def spread(parts):
        return [parts[0]] + [lax.ppermute(parts[d], "shard", xor_perm(shards, d)) for d in range(1, shards)]

    xs = gather_plane(tokens)
    cots = gather_plane(cotangent)
    macs = nj * count * width * hidden_width * 2
    total = pltpu.VMEM((nj, count, hidden_width), F32)
    joined = pltpu.VMEM((nj, count, hidden_width), BF)
    acc = pltpu.VMEM((hidden_width, width), F32)
    dense = shape((width, hidden_width), BF)

    def part_shapes(slots):
        dims = (slots, nj, part, hidden_width)
        return [shape(dims, F32)] + [shape(dims, BF)] * (shards - 1)

    *gate_up, gate_dense, up_dense = call(
        functools.partial(gate_up_kernel, shards, nj),
        [z_arr, g_rows, u_rows],
        [*xs, my_gate_blocks, my_up_blocks],
        part_shapes(2) + [dense, dense],
        [total, total],
        2 * macs,
        "gate_up",
    )
    *hidden_grads, down_dense = call(
        functools.partial(hidden_grad_kernel, shards, nj),
        [z_arr, d_rows],
        [*cots, my_down_blocks],
        part_shapes(1) + [shape((hidden_width, width), BF)],
        [total],
        macs,
        "hidden_grad",
    )
    gate_up = spread(gate_up)
    hidden_grads = spread(hidden_grads)
    act = shape((nj, part, hidden_width), BF)
    sums, hidden = call(
        hidden_kernel, [], gate_up, [shape((2, nj, part, hidden_width), F32), act], [], macs // 64, "hidden"
    )
    gate_act, up_act = call(act_grad_kernel, [], [sums, *hidden_grads], [act, act], [], macs // 64, "act_grad")
    hiddens = spread([hidden] * shards)
    gate_acts = spread([gate_act] * shards)
    up_acts = spread([up_act] * shards)

    plane_shapes = [shape((n_dp, count, width), F32)] + [shape((n_tok - 1, count, width), BF)] * n_dp
    grad_shape = shape((columns, per_owner, size, size), BF)
    keep_mixed, *rest = call(
        functools.partial(mixed_kernel, shards, nj, n_tok),
        [z_arr, d_rows],
        [*hiddens, down_dense, *cots],
        plane_shapes + [grad_shape],
        [joined, acc],
        2 * macs,
        "mixed",
    )
    send_mixed, down_grad = rest[:-1], rest[-1]
    gate_grad, joined_gate = call(
        functools.partial(gate_grad_kernel, shards, nj),
        [z_arr, g_rows],
        [*gate_acts, *xs],
        [grad_shape, shape((nj, count, hidden_width), BF)],
        [acc],
        macs,
        "gate_grad",
    )
    keep_tokens, *rest = call(
        functools.partial(tokens_grad_kernel, shards, nj, n_tok),
        [z_arr, u_rows],
        [*up_acts, joined_gate, gate_dense, up_dense, *xs],
        plane_shapes + [grad_shape],
        [joined, acc],
        3 * macs,
        "tokens_grad",
    )
    send_tokens, up_grad = rest[:-1], rest[-1]

    def sum_plane(keep, send):
        final = None
        for dx in reversed(range(n_dp)):
            term = keep[dx]
            for dc in range(1, n_tok):
                term += lax.ppermute(send[dx][dc - 1], "tok", xor_perm(n_tok, dc)).astype(F32)
            if dx:
                term = lax.ppermute(term.astype(BF), "dp", xor_perm(n_dp, dx)).astype(F32)
            final = term if final is None else final + term
        return final.astype(BF)

    g_perm = grad_perm(shards, n_dp, n_tok)
    home = lambda a: lax.ppermute(a, PLANE, g_perm)
    return (
        sum_plane(keep_mixed, send_mixed),
        sum_plane(keep_tokens, send_tokens),
        home(gate_grad),
        home(up_grad),
        home(down_grad),
    )


def solution(mesh):
    shards, n_dp, n_tok = (mesh.shape[name] for name in PLANE)
    assert shards == n_dp * n_tok
    in_specs = (
        P(("groups", "dp", "tok"), "shard"),
        P("shard", None, None, None),
        P("shard", None, None, None),
        P("shard", None, None, None),
        P("shard", None),
        P("shard", None),
        P(),
        P(("groups", "dp", "tok"), "shard"),
    )
    out_specs = (
        P(("groups", "dp", "tok"), "shard"),
        P(("groups", "dp", "tok"), "shard"),
        P(("groups", "shard"), ("dp", "tok"), None, None),
        P(("groups", "shard"), ("dp", "tok"), None, None),
        P(("groups", "shard"), ("dp", "tok"), None, None),
    )
    program = functools.partial(body, n_dp, n_tok, shards)
    return jax.shard_map(program, mesh=mesh, in_specs=in_specs, out_specs=out_specs, check_vma=False)
```

```python
import functools

import jax
import jax.numpy as jnp
from jax import lax
from jax.experimental import pallas as pl
from jax.experimental.pallas import tpu as pltpu
from jax.sharding import PartitionSpec as P

BF = jnp.bfloat16
F32 = jnp.float32
LIMIT = 16 << 20
Z, Q, OWNER, OWNED = range(4)
PLANE = ("shard", "dp", "tok")


def xor_perm(count, step):
    return [(i, i ^ step) for i in range(count)]


def weight_perm(shards, n_dp, n_tok):
    pairs = []
    for z in range(shards):
        for x in range(n_dp):
            for c in range(n_tok):
                q = c * n_dp + x
                pairs.append((q * n_dp * n_tok + weight_source(shards, n_dp, n_tok, q, z), (z * n_dp + x) * n_tok + c))
    return pairs


def weight_source(shards, n_dp, n_tok, q, z):
    if (shards, n_dp, n_tok) == (4, 2, 2):
        x = q % 2
        far = (q < 2) != (z < 2)
        return (x if far else 1 - x) * 2 + z % 2
    return z


def weight_owner(shards, n_dp, n_tok, q, x, c):
    if (shards, n_dp, n_tok) == (4, 2, 2):
        far = (x == (q & 1)).astype(jnp.int32)
        return ((q >> 1) ^ far) * 2 + c
    return x * n_tok + c


def grad_perm(shards, n_dp, n_tok):
    return [
        ((z * n_dp + x) * n_tok + c, (c * n_dp + x) * n_dp * n_tok + z)
        for z in range(shards)
        for x in range(n_dp)
        for c in range(n_tok)
    ]


def vmem(count):
    return [pl.BlockSpec(memory_space=pltpu.VMEM)] * count


def smem(count):
    return [pl.BlockSpec(memory_space=pltpu.SMEM)] * count


def call(kernel, scalars, arrays, outs, scratch, flops, kept, limit, out_spaces):
    moved = sum(a.size * a.dtype.itemsize for a in (*arrays, *kept))
    moved += sum(o.size * o.dtype.itemsize for o in outs)
    return pl.pallas_call(
        kernel,
        out_shape=outs,
        in_specs=smem(len(scalars)) + vmem(len(arrays)) + [pl.BlockSpec(memory_space=pltpu.HBM)] * len(kept),
        out_specs=[pl.BlockSpec(memory_space=s) for s in out_spaces] if out_spaces else vmem(len(outs)),
        scratch_shapes=scratch,
        compiler_params=pltpu.CompilerParams(vmem_limit_bytes=limit),
        cost_estimate=pl.CostEstimate(flops=flops, bytes_accessed=moved, transcendentals=0),
    )(*scalars, *arrays, *kept)


def aligned(value, size):
    return pl.multiple_of(value * size, size)


def down_places(info, down_rows, columns, per_owner):
    first_row, first = info[Q] * columns, info[Z] * per_owner
    return lambda c, k: down_rows[first_row + c, first + k] - info[Z] * info[OWNED]


def scatter_cols(dense, packed, place, columns):
    count, size, _ = packed.shape
    per_owner = count // columns
    dense[...] = jnp.zeros_like(dense)
    for c in range(columns):
        for k in range(per_owner):
            here = pl.ds(aligned(place(c, k), size), size)
            dense[c * size : (c + 1) * size, here] = packed[c * per_owner + k]


def split_rows(total, r, slot, outs, z):
    rows = outs[0].shape[2]
    for d, out in enumerate(outs):
        out[slot, r] = total[r, pl.ds(aligned(z ^ d, rows), rows), :].astype(out.dtype)


def copy_owner(pairs, owner, sems):
    copies = []
    for i, (source, target) in enumerate(pairs):
        columns = source.shape[0]
        per_owner = target.shape[0] // columns
        for c in range(columns):
            part = source.at[c, pl.ds(owner * per_owner, per_owner)]
            place = target.at[pl.ds(c * per_owner, per_owner)]
            copies.append(pltpu.make_async_copy(part, place, sems.at[i * columns + c]))
    for copy in copies:
        copy.start()
    return copies


def pack_kernel(info, gate_rows, up_rows, gate, up, down, rows_out, gate_out, up_out, down_out, sems):
    copies = copy_owner([(gate, gate_out), (up, up_out), (down, down_out)], info[OWNER], sems)
    columns, per_owner = rows_out.shape[1:]
    for i, rows in enumerate((gate_rows, up_rows)):
        for c in range(columns):
            for k in range(per_owner):
                rows_out[i, c, k] = rows[c, info[OWNER] * per_owner + k] - info[OWNER] * info[OWNED]
    for copy in copies:
        copy.wait()


def scatter_rows(dense, packed, rows, i):
    columns, per_owner = rows.shape[1:]
    size = packed.shape[1]
    dense[...] = jnp.zeros_like(dense)
    for c in range(columns):
        for k in range(per_owner):
            place = pl.ds(aligned(rows[i, c, k], size), size)
            dense[place, c * size : (c + 1) * size] = packed[c * per_owner + k]


def own_kernel(shards, n, i, info, rows, *refs):
    xs, packed = refs[:n], refs[n]
    outs = refs[n + 1 : n + 1 + shards]
    dense, total = refs[n + 1 + shards :]
    scatter_rows(dense, packed, rows, i)
    for r, x in enumerate(xs):
        total[r] = jnp.dot(x[...], dense[...], preferred_element_type=F32)
        split_rows(total, r, 0, outs, info[Z])


def other_gate_up_kernel(shards, n, info, *refs):
    outs = refs[n + 2 : n + 2 + shards]
    gate_up(info[Z], refs[:n], refs[n], refs[n + 1], outs, *refs[n + 2 + shards :])


def gate_up(z, xs, gate_dense, up_dense, outs, gate_total, up_total):
    for r, x in enumerate(xs):
        gate_total[r] = jnp.dot(x[...], gate_dense[...], preferred_element_type=F32)
        split_rows(gate_total, r, 0, outs, z)
        up_total[r] = jnp.dot(x[...], up_dense[...], preferred_element_type=F32)
        split_rows(up_total, r, 1, outs, z)


def hidden_grad_kernel(shards, nj, columns, info, down_rows, *refs):
    cots = refs[:nj]
    down_blocks = refs[nj]
    outs = refs[nj + 1 : nj + 1 + shards]
    down_dense, total = refs[nj + 1 + shards :]
    place = down_places(info, down_rows, columns, down_blocks.shape[0] // columns)
    scatter_cols(down_dense, down_blocks, place, columns)
    for r in range(nj):
        total[r] = lax.dot_general(
            cots[r][...], down_dense[...], (((1,), (1,)), ((), ())), preferred_element_type=F32
        )
        split_rows(total, r, 0, outs, info[Z])


def hidden_kernel(shards, *refs):
    gates, ups, others = (refs[i * shards : (i + 1) * shards] for i in range(3))
    sums, hidden = refs[3 * shards :]
    first = gates[0].shape[1]
    total = lambda parts, slot: sum(part[slot].astype(F32) for part in parts)
    for start, gate, up in (
        (0, total(gates, 0), total(ups, 0)),
        (first, total(others, 0), total(others, 1)),
    ):
        here = pl.ds(start, gate.shape[0])
        sums[0, here] = gate
        sums[1, here] = up
        hidden[here] = (gate * jax.nn.sigmoid(gate) * up).astype(BF)


def act_grad_kernel(sums, *refs):
    parts, (gate_act, up_act) = refs[:-2], refs[-2:]
    hidden_grad = sum(part[0].astype(F32) for part in parts)
    gate, up = sums[0], sums[1]
    s = jax.nn.sigmoid(gate)
    gate_act[...] = (hidden_grad * up * s * (1.0 + gate * (1.0 - s))).astype(BF)
    up_act[...] = (hidden_grad * (gate * s)).astype(BF)


def join_rows(joined, parts, z):
    rows = parts[0].shape[1]
    for r in range(joined.shape[0]):
        for d, part in enumerate(parts):
            joined[r, pl.ds(aligned(z ^ d, rows), rows), :] = part[r]


def weight_grad(acc, left, rights, stage, sems):
    copies = [pltpu.make_async_copy(right, stage.at[r], sems.at[r]) for r, right in enumerate(rights)]
    for copy in copies:
        copy.start()
    for r, copy in enumerate(copies):
        copy.wait()
        term = lax.dot_general(left[r], stage[r], (((0,), (0,)), ((), ())), preferred_element_type=F32)
        if r == 0:
            acc[...] = term
        else:
            acc[...] += term


def pick_blocks(out, acc, place, transposed):
    columns, per_owner, size, _ = out.shape
    for c in range(columns):
        for k in range(per_owner):
            block = acc[c * size : (c + 1) * size, pl.ds(aligned(place(c, k), size), size)]
            out[c, k] = (block.T if transposed else block).astype(BF)


def put_plane(keep, send, r, n_tok, value):
    dx, dc = divmod(r, n_tok)
    if dc == 0:
        keep[dx][...] = value
    else:
        send[dx][dc - 1] = value.astype(BF)


def sum_kernel(first, *refs):
    *others, out = refs
    total = first[...]
    for other in others:
        value = other[...].astype(F32)
        total += value if value.ndim == total.ndim else jnp.sum(value, axis=0)
    out[...] = total.astype(BF)


def deliver_kernel(*refs):
    count = len(refs) // 2
    for source, out in zip(refs[:count], refs[count:]):
        out[...] = source[...]


def mixed_kernel(shards, n_dp, n_tok, info, *refs):
    hiddens, dense = refs[:shards], refs[shards]
    keep, send = refs[shards + 1 : shards + 1 + n_dp], refs[shards + 1 + n_dp : shards + 1 + 2 * n_dp]
    joined = refs[shards + 1 + 2 * n_dp]
    join_rows(joined, hiddens, info[Z])
    for r in reversed(range(joined.shape[0])):
        put_plane(keep, send, r, n_tok, jnp.dot(joined[r], dense[...], preferred_element_type=F32))


def down_grad_kernel(info, down_rows, joined, *refs):
    *rights, grad, acc, stage, sems = refs
    weight_grad(acc, joined, rights, stage, sems)
    pick_blocks(grad, acc, down_places(info, down_rows, *grad.shape[:2]), False)


def up_grad_kernel(rows, joined, *refs):
    *rights, grad, acc, stage, sems = refs
    weight_grad(acc, joined, rights, stage, sems)
    pick_blocks(grad, acc, lambda c, k: rows[1, c, k], True)


def gate_grad_kernel(shards, nj, info, rows, *refs):
    acts = refs[:shards]
    xs = refs[shards : shards + nj]
    grad, joined, acc, stage, sems = refs[shards + nj :]
    join_rows(joined, acts, info[Z])
    weight_grad(acc, joined, xs, stage, sems)
    pick_blocks(grad, acc, lambda c, k: rows[0, c, k], True)


def tokens_grad_kernel(shards, n_dp, n_tok, info, *refs):
    acts = refs[:shards]
    joined_gate, gate_dense, up_dense = refs[shards : shards + 3]
    keep, send = refs[shards + 3 : shards + 3 + n_dp], refs[shards + 3 + n_dp : shards + 3 + 2 * n_dp]
    joined = refs[shards + 3 + 2 * n_dp]
    join_rows(joined, acts, info[Z])
    contract = (((1,), (1,)), ((), ()))
    for r in reversed(range(joined.shape[0])):
        value = lax.dot_general(joined_gate[r], gate_dense[...], contract, preferred_element_type=F32)
        value += lax.dot_general(joined[r], up_dense[...], contract, preferred_element_type=F32)
        put_plane(keep, send, r, n_tok, value)


def shape(dims, dtype):
    return jax.ShapeDtypeStruct(dims, dtype)


def body(n_dp, n_tok, shards, tokens, gate_blocks, up_blocks, down_blocks, gate_rows, up_rows, down_rows, cotangent):
    nj = n_dp * n_tok
    z = lax.axis_index("shard")
    x_index, c_index = lax.axis_index("dp"), lax.axis_index("tok")
    q = c_index * n_dp + x_index
    count, width = tokens.shape
    columns, nonzero, size, _ = gate_blocks.shape
    per_owner = nonzero // shards
    owned = width // size
    hidden_width = columns * size
    part = count // shards
    blocks = columns * per_owner

    def spread(parts):
        return [parts[0]] + [lax.ppermute(parts[d], "shard", xor_perm(shards, d)) for d in range(1, shards)]

    def run(kernel, scalars, arrays, outs, scratch, flops, kept=(), limit=LIMIT, out_spaces=None):
        return call(kernel, scalars, arrays, outs, scratch, flops, kept, limit, out_spaces)

    def gather_plane(own):
        groups = []
        for dx in range(n_dp):
            base = own if dx == 0 else lax.ppermute(own, "dp", xor_perm(n_dp, dx))
            group = [base]
            for dc in range(1, n_tok):
                group.append(lax.ppermute(base, "tok", xor_perm(n_tok, dc)))
            groups.append(group)
        return groups[0], [a for group in groups[1:] for a in group]

    w_perm = weight_perm(shards, n_dp, n_tok)
    owner = weight_owner(shards, n_dp, n_tok, z, x_index, c_index)
    info = jnp.stack([v.astype(jnp.int32) for v in (z, q, owner, jnp.int32(owned))])
    packed_shape = shape((blocks, size, size), BF)
    rows, gate_part, up_part, down_part = run(
        pack_kernel,
        [info, gate_rows, up_rows],
        [],
        [shape((2, columns, per_owner), jnp.int32)] + [packed_shape] * 3,
        [pltpu.SemaphoreType.DMA((3 * columns,))],
        0,
        [gate_blocks, up_blocks, down_blocks],
        60 << 20,
        [pltpu.SMEM] + [pltpu.VMEM] * 3,
    )
    gate_part = lax.ppermute(gate_part, PLANE, w_perm)
    rows = lax.ppermute(rows, PLANE, w_perm)
    up_part = lax.ppermute(up_part, PLANE, w_perm)
    down_part = lax.ppermute(down_part, PLANE, w_perm)

    own_x, other_x = gather_plane(tokens)
    own_c, other_c = gather_plane(cotangent)
    xs, cots = own_x + other_x, own_c + other_c
    macs = nj * count * width * hidden_width * 2
    joined = pltpu.VMEM((nj, count, hidden_width), BF)
    joined_shape = shape((nj, count, hidden_width), BF)
    acc = pltpu.VMEM((hidden_width, width), F32)
    dense = shape((width, hidden_width), BF)

    def part_shapes(slots, n):
        dims = (slots, n, part, hidden_width)
        return [shape(dims, F32)] + [shape(dims, BF)] * (shards - 1)

    def totals(n):
        return pltpu.VMEM((n, count, hidden_width), F32)

    def own(i, blocks_part):
        return run(
            functools.partial(own_kernel, shards, n_tok, i),
            [info, rows],
            [*own_x, blocks_part],
            part_shapes(1, n_tok) + [dense],
            [totals(n_tok)],
            macs // n_dp,
        )

    *gate0, gate_dense = own(0, gate_part)
    gate0 = spread(gate0)
    *up0, up_dense = own(1, up_part)
    up0 = spread(up0)
    gate_up1 = run(
        functools.partial(other_gate_up_kernel, shards, nj - n_tok),
        [info],
        [*other_x, gate_dense, up_dense],
        part_shapes(2, nj - n_tok),
        [totals(nj - n_tok)] * 2,
        2 * macs * (n_dp - 1) // n_dp,
    )
    gate_up1 = spread(gate_up1)
    *hidden_grads, down_dense = run(
        functools.partial(hidden_grad_kernel, shards, nj, columns),
        [info, down_rows],
        [*cots, down_part],
        part_shapes(1, nj) + [shape((hidden_width, width), BF)],
        [totals(nj)],
        macs,
    )
    hidden_grads = spread(hidden_grads)
    act = shape((nj, part, hidden_width), BF)
    sums, hidden = run(
        functools.partial(hidden_kernel, shards),
        [],
        [*gate0, *up0, *gate_up1],
        [shape((2, nj, part, hidden_width), F32), act],
        [],
        macs // 64,
    )
    hiddens = spread([hidden] * shards)
    gate_act, up_act = run(act_grad_kernel, [], [sums, *hidden_grads], [act, act], [], macs // 64)
    gate_acts = spread([gate_act] * shards)
    up_acts = spread([up_act] * shards)

    plane_shapes = [shape((count, width), F32)] * n_dp + [shape((n_tok - 1, count, width), BF)] * n_dp
    grad_shape = shape((columns, per_owner, size, size), BF)
    *mixed, joined_hidden = run(
        functools.partial(mixed_kernel, shards, n_dp, n_tok),
        [info],
        [*hiddens, down_dense],
        plane_shapes + [joined_shape],
        [],
        macs,
    )
    staged = [acc, pltpu.VMEM((nj, count, width), BF), pltpu.SemaphoreType.DMA((nj,))]
    (down_grad,) = run(down_grad_kernel, [info, down_rows], [joined_hidden], [grad_shape], staged, macs, cots)
    gate_grad, joined_gate = run(
        functools.partial(gate_grad_kernel, shards, nj),
        [info, rows],
        gate_acts,
        [grad_shape, joined_shape],
        staged,
        macs,
        xs,
    )
    *tokens_terms, joined_up = run(
        functools.partial(tokens_grad_kernel, shards, n_dp, n_tok),
        [info],
        [*up_acts, joined_gate, gate_dense, up_dense],
        plane_shapes + [joined_shape],
        [],
        2 * macs,
    )
    (up_grad,) = run(up_grad_kernel, [rows], [joined_up], [grad_shape], staged, macs, xs)

    def sum_plane(terms):
        arrived = []
        total = lambda parts: run(sum_kernel, [], parts, [shape((count, width), BF)], [], 0)[0]
        for dx in reversed(range(n_dp)):
            parts = [terms[dx]]
            if n_tok == 2:
                parts.append(lax.ppermute(terms[n_dp + dx], "tok", xor_perm(n_tok, 1)))
            else:
                for dc in range(1, n_tok):
                    parts.append(lax.ppermute(terms[n_dp + dx][dc - 1], "tok", xor_perm(n_tok, dc)))
            if dx:
                arrived.append(lax.ppermute(total(parts), "dp", xor_perm(n_dp, dx)))
        return total(parts + arrived)

    g_perm = grad_perm(shards, n_dp, n_tok)

    def home(grad):
        grad = lax.ppermute(grad, PLANE, g_perm)
        return run(deliver_kernel, [], [grad], [grad_shape], [], 0)[0]

    return (sum_plane(mixed), sum_plane(tokens_terms), home(gate_grad), home(up_grad), home(down_grad))


def solution(mesh):
    shards, n_dp, n_tok = (mesh.shape[name] for name in PLANE)
    assert shards == n_dp * n_tok
    in_specs = (
        P(("groups", "dp", "tok"), "shard"),
        P("shard", None, None, None),
        P("shard", None, None, None),
        P("shard", None, None, None),
        P("shard", None),
        P("shard", None),
        P(),
        P(("groups", "dp", "tok"), "shard"),
    )
    out_specs = (
        P(("groups", "dp", "tok"), "shard"),
        P(("groups", "dp", "tok"), "shard"),
        P(("groups", "shard"), ("dp", "tok"), None, None),
        P(("groups", "shard"), ("dp", "tok"), None, None),
        P(("groups", "shard"), ("dp", "tok"), None, None),
    )
    program = functools.partial(body, n_dp, n_tok, shards)
    return jax.shard_map(program, mesh=mesh, in_specs=in_specs, out_specs=out_specs, check_vma=False)
```

```python
import functools

import jax
import jax.numpy as jnp
from jax import lax
from jax.experimental import pallas as pl
from jax.experimental.pallas import tpu as pltpu
from jax.sharding import PartitionSpec as P

BF = jnp.bfloat16
F32 = jnp.float32
LIMIT = 16 << 20
Z, Q, OWNER, OWNED = range(4)
PLANE = ("shard", "dp", "tok")


def xor_perm(count, step):
    return [(i, i ^ step) for i in range(count)]


def weight_perm(shards, n_dp, n_tok):
    pairs = []
    for z in range(shards):
        for x in range(n_dp):
            for c in range(n_tok):
                q = c * n_dp + x
                pairs.append((q * n_dp * n_tok + weight_source(shards, n_dp, n_tok, q, z), (z * n_dp + x) * n_tok + c))
    return pairs


def weight_source(shards, n_dp, n_tok, q, z):
    if (shards, n_dp, n_tok) == (4, 2, 2):
        x = q % 2
        far = (q < 2) != (z < 2)
        return (x if far else 1 - x) * 2 + z % 2
    return z


def weight_owner(shards, n_dp, n_tok, q, x, c):
    if (shards, n_dp, n_tok) == (4, 2, 2):
        far = (x == (q & 1)).astype(jnp.int32)
        return ((q >> 1) ^ far) * 2 + c
    return x * n_tok + c


def grad_perm(shards, n_dp, n_tok):
    return [
        ((z * n_dp + x) * n_tok + c, (c * n_dp + x) * n_dp * n_tok + z)
        for z in range(shards)
        for x in range(n_dp)
        for c in range(n_tok)
    ]


def vmem(count):
    return [pl.BlockSpec(memory_space=pltpu.VMEM)] * count


def smem(count):
    return [pl.BlockSpec(memory_space=pltpu.SMEM)] * count


def call(kernel, scalars, arrays, outs, scratch, flops, kept, limit, out_spaces):
    moved = sum(a.size * a.dtype.itemsize for a in (*arrays, *kept))
    moved += sum(o.size * o.dtype.itemsize for o in outs)
    return pl.pallas_call(
        kernel,
        out_shape=outs,
        in_specs=smem(len(scalars)) + vmem(len(arrays)) + [pl.BlockSpec(memory_space=pltpu.HBM)] * len(kept),
        out_specs=[pl.BlockSpec(memory_space=s) for s in out_spaces] if out_spaces else vmem(len(outs)),
        scratch_shapes=scratch,
        compiler_params=pltpu.CompilerParams(vmem_limit_bytes=limit),
        cost_estimate=pl.CostEstimate(flops=flops, bytes_accessed=moved, transcendentals=0),
    )(*scalars, *arrays, *kept)


def aligned(value, size):
    return pl.multiple_of(value * size, size)


def down_places(info, down_rows, columns, per_owner):
    first_row, first = info[Q] * columns, info[Z] * per_owner
    return lambda c, k: down_rows[first_row + c, first + k] - info[Z] * info[OWNED]


def scatter_cols(dense, packed, place, columns):
    count, size, _ = packed.shape
    per_owner = count // columns
    dense[...] = jnp.zeros_like(dense)
    for c in range(columns):
        for k in range(per_owner):
            here = pl.ds(aligned(place(c, k), size), size)
            dense[c * size : (c + 1) * size, here] = packed[c * per_owner + k]


def split_rows(total, r, slot, outs, z):
    rows = outs[0].shape[2]
    for d, out in enumerate(outs):
        out[slot, r] = total[r, pl.ds(aligned(z ^ d, rows), rows), :].astype(out.dtype)


def copy_owner(pairs, owner, sems):
    copies = []
    for i, (source, target) in enumerate(pairs):
        columns = source.shape[0]
        per_owner = target.shape[0] // columns
        for c in range(columns):
            part = source.at[c, pl.ds(owner * per_owner, per_owner)]
            place = target.at[pl.ds(c * per_owner, per_owner)]
            copies.append(pltpu.make_async_copy(part, place, sems.at[i * columns + c]))
    for copy in copies:
        copy.start()
    return copies


def pack_kernel(info, gate_rows, up_rows, gate, up, down, rows_out, gate_out, up_out, down_out, sems):
    copies = copy_owner([(gate, gate_out), (up, up_out), (down, down_out)], info[OWNER], sems)
    columns, per_owner = rows_out.shape[1:]
    for i, rows in enumerate((gate_rows, up_rows)):
        for c in range(columns):
            for k in range(per_owner):
                rows_out[i, c, k] = rows[c, info[OWNER] * per_owner + k] - info[OWNER] * info[OWNED]
    for copy in copies:
        copy.wait()


def scatter_rows(dense, packed, rows, i):
    columns, per_owner = rows.shape[1:]
    size = packed.shape[1]
    dense[...] = jnp.zeros_like(dense)
    for c in range(columns):
        for k in range(per_owner):
            place = pl.ds(aligned(rows[i, c, k], size), size)
            dense[place, c * size : (c + 1) * size] = packed[c * per_owner + k]


def own_kernel(shards, n, i, info, rows, *refs):
    xs, packed = refs[:n], refs[n]
    outs = refs[n + 1 : n + 1 + shards]
    dense, total = refs[n + 1 + shards :]
    scatter_rows(dense, packed, rows, i)
    for r, x in enumerate(xs):
        total[r] = jnp.dot(x[...], dense[...], preferred_element_type=F32)
        split_rows(total, r, 0, outs, info[Z])


def other_gate_up_kernel(shards, n, info, *refs):
    outs = refs[n + 2 : n + 2 + shards]
    gate_up(info[Z], refs[:n], refs[n], refs[n + 1], outs, *refs[n + 2 + shards :])


def gate_up(z, xs, gate_dense, up_dense, outs, gate_total, up_total):
    for r, x in enumerate(xs):
        gate_total[r] = jnp.dot(x[...], gate_dense[...], preferred_element_type=F32)
        split_rows(gate_total, r, 0, outs, z)
        up_total[r] = jnp.dot(x[...], up_dense[...], preferred_element_type=F32)
        split_rows(up_total, r, 1, outs, z)


def hidden_grad_kernel(shards, nj, columns, info, down_rows, *refs):
    cots = refs[:nj]
    down_blocks = refs[nj]
    outs = refs[nj + 1 : nj + 1 + shards]
    down_dense, total = refs[nj + 1 + shards :]
    place = down_places(info, down_rows, columns, down_blocks.shape[0] // columns)
    scatter_cols(down_dense, down_blocks, place, columns)
    for r in range(nj):
        total[r] = lax.dot_general(
            cots[r][...], down_dense[...], (((1,), (1,)), ((), ())), preferred_element_type=F32
        )
        split_rows(total, r, 0, outs, info[Z])


def hidden_kernel(shards, *refs):
    gates, ups, others = (refs[i * shards : (i + 1) * shards] for i in range(3))
    sums, hidden = refs[3 * shards :]
    first = gates[0].shape[1]
    total = lambda parts, slot: sum(part[slot].astype(F32) for part in parts)
    for start, gate, up in (
        (0, total(gates, 0), total(ups, 0)),
        (first, total(others, 0), total(others, 1)),
    ):
        here = pl.ds(start, gate.shape[0])
        sums[0, here] = gate
        sums[1, here] = up
        hidden[here] = (gate * jax.nn.sigmoid(gate) * up).astype(BF)


def act_grad_kernel(sums, *refs):
    parts, (gate_act, up_act) = refs[:-2], refs[-2:]
    hidden_grad = sum(part[0].astype(F32) for part in parts)
    gate, up = sums[0], sums[1]
    s = jax.nn.sigmoid(gate)
    gate_act[...] = (hidden_grad * up * s * (1.0 + gate * (1.0 - s))).astype(BF)
    up_act[...] = (hidden_grad * (gate * s)).astype(BF)


def join_rows(joined, parts, z):
    rows = parts[0].shape[1]
    for r in range(joined.shape[0]):
        for d, part in enumerate(parts):
            joined[r, pl.ds(aligned(z ^ d, rows), rows), :] = part[r]


def weight_grad(acc, left, rights, stage, sems):
    copies = [pltpu.make_async_copy(right, stage.at[r], sems.at[r]) for r, right in enumerate(rights)]
    for copy in copies:
        copy.start()
    for r, copy in enumerate(copies):
        copy.wait()
        term = lax.dot_general(left[r], stage[r], (((0,), (0,)), ((), ())), preferred_element_type=F32)
        if r == 0:
            acc[...] = term
        else:
            acc[...] += term


def pick_blocks(out, acc, place, transposed):
    columns, per_owner, size, _ = out.shape
    for c in range(columns):
        for k in range(per_owner):
            block = acc[c * size : (c + 1) * size, pl.ds(aligned(place(c, k), size), size)]
            out[c, k] = (block.T if transposed else block).astype(BF)


def put_plane(keep, send, r, n_tok, value):
    dx, dc = divmod(r, n_tok)
    if dc == 0:
        keep[dx][...] = value
    else:
        send[dx][dc - 1] = value.astype(BF)


def sum_kernel(first, *refs):
    *others, out = refs
    total = first[...]
    for other in others:
        value = other[...].astype(F32)
        total += value if value.ndim == total.ndim else jnp.sum(value, axis=0)
    out[...] = total.astype(BF)


def deliver_kernel(*refs):
    count = len(refs) // 2
    for source, out in zip(refs[:count], refs[count:]):
        out[...] = source[...]


def mixed_kernel(shards, n_dp, n_tok, info, *refs):
    hiddens, dense = refs[:shards], refs[shards]
    keep, send = refs[shards + 1 : shards + 1 + n_dp], refs[shards + 1 + n_dp : shards + 1 + 2 * n_dp]
    joined = refs[shards + 1 + 2 * n_dp]
    join_rows(joined, hiddens, info[Z])
    for r in reversed(range(joined.shape[0])):
        put_plane(keep, send, r, n_tok, jnp.dot(joined[r], dense[...], preferred_element_type=F32))


def down_grad_kernel(info, down_rows, joined, *refs):
    *rights, grad, acc, stage, sems = refs
    weight_grad(acc, joined, rights, stage, sems)
    pick_blocks(grad, acc, down_places(info, down_rows, *grad.shape[:2]), False)


def up_grad_kernel(rows, joined, *refs):
    *rights, grad, acc, stage, sems = refs
    weight_grad(acc, joined, rights, stage, sems)
    pick_blocks(grad, acc, lambda c, k: rows[1, c, k], True)


def gate_grad_kernel(shards, nj, info, rows, *refs):
    acts = refs[:shards]
    xs = refs[shards : shards + nj]
    grad, joined, acc, stage, sems = refs[shards + nj :]
    join_rows(joined, acts, info[Z])
    weight_grad(acc, joined, xs, stage, sems)
    pick_blocks(grad, acc, lambda c, k: rows[0, c, k], True)


def tokens_grad_kernel(shards, n_dp, n_tok, info, *refs):
    acts = refs[:shards]
    joined_gate, gate_dense, up_dense = refs[shards : shards + 3]
    keep, send = refs[shards + 3 : shards + 3 + n_dp], refs[shards + 3 + n_dp : shards + 3 + 2 * n_dp]
    joined = refs[shards + 3 + 2 * n_dp]
    join_rows(joined, acts, info[Z])
    contract = (((1,), (1,)), ((), ()))
    for r in reversed(range(joined.shape[0])):
        value = lax.dot_general(joined_gate[r], gate_dense[...], contract, preferred_element_type=F32)
        value += lax.dot_general(joined[r], up_dense[...], contract, preferred_element_type=F32)
        put_plane(keep, send, r, n_tok, value)


def shape(dims, dtype):
    return jax.ShapeDtypeStruct(dims, dtype)


def body(n_dp, n_tok, shards, tokens, gate_blocks, up_blocks, down_blocks, gate_rows, up_rows, down_rows, cotangent):
    nj = n_dp * n_tok
    z = lax.axis_index("shard")
    x_index, c_index = lax.axis_index("dp"), lax.axis_index("tok")
    q = c_index * n_dp + x_index
    count, width = tokens.shape
    columns, nonzero, size, _ = gate_blocks.shape
    per_owner = nonzero // shards
    owned = width // size
    hidden_width = columns * size
    part = count // shards
    blocks = columns * per_owner

    def spread(parts):
        return [parts[0]] + [lax.ppermute(parts[d], "shard", xor_perm(shards, d)) for d in range(1, shards)]

    def gather(own):
        have = {0: own}
        bit = shards // 2
        while bit:
            for d in sorted(have):
                have[d ^ bit] = lax.ppermute(have[d], "shard", xor_perm(shards, bit))
            bit //= 2
        return [have[d] for d in range(shards)]

    def run(kernel, scalars, arrays, outs, scratch, flops, kept=(), limit=LIMIT, out_spaces=None):
        return call(kernel, scalars, arrays, outs, scratch, flops, kept, limit, out_spaces)

    def gather_plane(own):
        groups = []
        for dx in range(n_dp):
            base = own if dx == 0 else lax.ppermute(own, "dp", xor_perm(n_dp, dx))
            group = [base]
            for dc in range(1, n_tok):
                group.append(lax.ppermute(base, "tok", xor_perm(n_tok, dc)))
            groups.append(group)
        return groups[0], [a for group in groups[1:] for a in group]

    w_perm = weight_perm(shards, n_dp, n_tok)
    owner = weight_owner(shards, n_dp, n_tok, z, x_index, c_index)
    info = jnp.stack([v.astype(jnp.int32) for v in (z, q, owner, jnp.int32(owned))])
    packed_shape = shape((blocks, size, size), BF)
    rows, gate_part, up_part, down_part = run(
        pack_kernel,
        [info, gate_rows, up_rows],
        [],
        [shape((2, columns, per_owner), jnp.int32)] + [packed_shape] * 3,
        [pltpu.SemaphoreType.DMA((3 * columns,))],
        0,
        [gate_blocks, up_blocks, down_blocks],
        60 << 20,
        [pltpu.SMEM] + [pltpu.VMEM] * 3,
    )
    gate_part = lax.ppermute(gate_part, PLANE, w_perm)
    rows = lax.ppermute(rows, PLANE, w_perm)
    up_part = lax.ppermute(up_part, PLANE, w_perm)
    down_part = lax.ppermute(down_part, PLANE, w_perm)

    own_x, other_x = gather_plane(tokens)
    own_c, other_c = gather_plane(cotangent)
    xs, cots = own_x + other_x, own_c + other_c
    macs = nj * count * width * hidden_width * 2
    joined = pltpu.VMEM((nj, count, hidden_width), BF)
    joined_shape = shape((nj, count, hidden_width), BF)
    acc = pltpu.VMEM((hidden_width, width), F32)
    dense = shape((width, hidden_width), BF)

    def part_shapes(slots, n):
        dims = (slots, n, part, hidden_width)
        return [shape(dims, F32)] + [shape(dims, BF)] * (shards - 1)

    def totals(n):
        return pltpu.VMEM((n, count, hidden_width), F32)

    def own(i, blocks_part):
        return run(
            functools.partial(own_kernel, shards, n_tok, i),
            [info, rows],
            [*own_x, blocks_part],
            part_shapes(1, n_tok) + [dense],
            [totals(n_tok)],
            macs // n_dp,
        )

    *gate0, gate_dense = own(0, gate_part)
    gate0 = spread(gate0)
    *up0, up_dense = own(1, up_part)
    up0 = spread(up0)
    gate_up1 = run(
        functools.partial(other_gate_up_kernel, shards, nj - n_tok),
        [info],
        [*other_x, gate_dense, up_dense],
        part_shapes(2, nj - n_tok),
        [totals(nj - n_tok)] * 2,
        2 * macs * (n_dp - 1) // n_dp,
    )
    gate_up1 = spread(gate_up1)
    *hidden_grads, down_dense = run(
        functools.partial(hidden_grad_kernel, shards, nj, columns),
        [info, down_rows],
        [*cots, down_part],
        part_shapes(1, nj) + [shape((hidden_width, width), BF)],
        [totals(nj)],
        macs,
    )
    hidden_grads = spread(hidden_grads)
    act = shape((nj, part, hidden_width), BF)
    sums, hidden = run(
        functools.partial(hidden_kernel, shards),
        [],
        [*gate0, *up0, *gate_up1],
        [shape((2, nj, part, hidden_width), F32), act],
        [],
        macs // 64,
    )
    hiddens = gather(hidden)
    gate_act, up_act = run(act_grad_kernel, [], [sums, *hidden_grads], [act, act], [], macs // 64)
    gate_acts = gather(gate_act)
    up_acts = gather(up_act)

    plane_shapes = [shape((count, width), F32)] * n_dp + [shape((n_tok - 1, count, width), BF)] * n_dp
    grad_shape = shape((columns, per_owner, size, size), BF)
    *mixed, joined_hidden = run(
        functools.partial(mixed_kernel, shards, n_dp, n_tok),
        [info],
        [*hiddens, down_dense],
        plane_shapes + [joined_shape],
        [],
        macs,
    )
    staged = [acc, pltpu.VMEM((nj, count, width), BF), pltpu.SemaphoreType.DMA((nj,))]
    (down_grad,) = run(down_grad_kernel, [info, down_rows], [joined_hidden], [grad_shape], staged, macs, cots)
    gate_grad, joined_gate = run(
        functools.partial(gate_grad_kernel, shards, nj),
        [info, rows],
        gate_acts,
        [grad_shape, joined_shape],
        staged,
        macs,
        xs,
    )
    *tokens_terms, joined_up = run(
        functools.partial(tokens_grad_kernel, shards, n_dp, n_tok),
        [info],
        [*up_acts, joined_gate, gate_dense, up_dense],
        plane_shapes + [joined_shape],
        [],
        2 * macs,
    )
    (up_grad,) = run(up_grad_kernel, [rows], [joined_up], [grad_shape], staged, macs, xs)

    def sum_plane(terms):
        arrived = []
        total = lambda parts: run(sum_kernel, [], parts, [shape((count, width), BF)], [], 0)[0]
        for dx in reversed(range(n_dp)):
            parts = [terms[dx]]
            if n_tok == 2:
                parts.append(lax.ppermute(terms[n_dp + dx], "tok", xor_perm(n_tok, 1)))
            else:
                for dc in range(1, n_tok):
                    parts.append(lax.ppermute(terms[n_dp + dx][dc - 1], "tok", xor_perm(n_tok, dc)))
            if dx:
                arrived.append(lax.ppermute(total(parts), "dp", xor_perm(n_dp, dx)))
        return total(parts + arrived)

    g_perm = grad_perm(shards, n_dp, n_tok)

    def home(grad):
        grad = lax.ppermute(grad, PLANE, g_perm)
        return run(deliver_kernel, [], [grad], [grad_shape], [], 0)[0]

    return (sum_plane(mixed), sum_plane(tokens_terms), home(gate_grad), home(up_grad), home(down_grad))


def solution(mesh):
    shards, n_dp, n_tok = (mesh.shape[name] for name in PLANE)
    assert shards == n_dp * n_tok
    in_specs = (
        P(("groups", "dp", "tok"), "shard"),
        P("shard", None, None, None),
        P("shard", None, None, None),
        P("shard", None, None, None),
        P("shard", None),
        P("shard", None),
        P(),
        P(("groups", "dp", "tok"), "shard"),
    )
    out_specs = (
        P(("groups", "dp", "tok"), "shard"),
        P(("groups", "dp", "tok"), "shard"),
        P(("groups", "shard"), ("dp", "tok"), None, None),
        P(("groups", "shard"), ("dp", "tok"), None, None),
        P(("groups", "shard"), ("dp", "tok"), None, None),
    )
    program = functools.partial(body, n_dp, n_tok, shards)
    return jax.shard_map(program, mesh=mesh, in_specs=in_specs, out_specs=out_specs, check_vma=False)
```

```python
import functools

import jax
import jax.numpy as jnp
from jax import lax
from jax.experimental import pallas as pl
from jax.experimental.pallas import tpu as pltpu
from jax.sharding import PartitionSpec as P

BF = jnp.bfloat16
F32 = jnp.float32
LIMIT = 16 << 20
Z, Q, OWNER, OWNED = range(4)
PLANE = ("shard", "dp", "tok")


def xor_perm(count, step):
    return [(i, i ^ step) for i in range(count)]


def column_shard(n_dp, z, x, c):
    return c * n_dp + (x ^ (z & 1))


def shard_perm(shards, n_dp, d):
    return [(z * n_dp + x, (z ^ d) * n_dp + (x ^ (d & 1))) for z in range(shards) for x in range(n_dp)]


def weight_perm(shards, n_dp, n_tok):
    pairs = []
    for z in range(shards):
        for x in range(n_dp):
            for c in range(n_tok):
                source = x * n_tok + z // 2 if (shards, n_dp, n_tok) == (4, 2, 2) else z
                plane = column_shard(n_dp, z, x, c) * n_dp * n_tok
                pairs.append((plane + source, (z * n_dp + x) * n_tok + c))
    return pairs


def weight_owner(shards, n_dp, n_tok, z, x, c):
    if (shards, n_dp, n_tok) == (4, 2, 2):
        return c * 2 + (x ^ (z & 1))
    return x * n_tok + c


def grad_perm(shards, n_dp, n_tok):
    return [
        ((z * n_dp + x) * n_tok + c, column_shard(n_dp, z, x, c) * n_dp * n_tok + z)
        for z in range(shards)
        for x in range(n_dp)
        for c in range(n_tok)
    ]


def vmem(count):
    return [pl.BlockSpec(memory_space=pltpu.VMEM)] * count


def smem(count):
    return [pl.BlockSpec(memory_space=pltpu.SMEM)] * count


def call(kernel, scalars, arrays, outs, scratch, flops, kept, limit, out_spaces):
    moved = sum(a.size * a.dtype.itemsize for a in (*arrays, *kept))
    moved += sum(o.size * o.dtype.itemsize for o in outs)
    return pl.pallas_call(
        kernel,
        out_shape=outs,
        in_specs=smem(len(scalars)) + vmem(len(arrays)) + [pl.BlockSpec(memory_space=pltpu.HBM)] * len(kept),
        out_specs=[pl.BlockSpec(memory_space=s) for s in out_spaces] if out_spaces else vmem(len(outs)),
        scratch_shapes=scratch,
        compiler_params=pltpu.CompilerParams(vmem_limit_bytes=limit),
        cost_estimate=pl.CostEstimate(flops=flops, bytes_accessed=moved, transcendentals=0),
    )(*scalars, *arrays, *kept)


def aligned(value, size):
    return pl.multiple_of(value * size, size)


def down_places(info, down_rows, columns, per_owner):
    first_row, first = info[Q] * columns, info[Z] * per_owner
    return lambda c, k: down_rows[first_row + c, first + k] - info[Z] * info[OWNED]


def scatter_cols(dense, packed, place, columns):
    count, size, _ = packed.shape
    per_owner = count // columns
    dense[...] = jnp.zeros_like(dense)
    for c in range(columns):
        for k in range(per_owner):
            here = pl.ds(aligned(place(c, k), size), size)
            dense[c * size : (c + 1) * size, here] = packed[c * per_owner + k]


def split_rows(total, r, near, far, z):
    rows = near.shape[2]
    for d in range(2 * near.shape[0]):
        out = far if d % 2 else near
        out[d // 2, r] = total[r, pl.ds(aligned(z ^ d, rows), rows), :].astype(out.dtype)


def copy_owner(pairs, owner, sems):
    copies = []
    for i, (source, target) in enumerate(pairs):
        columns = source.shape[0]
        per_owner = target.shape[0] // columns
        for c in range(columns):
            part = source.at[c, pl.ds(owner * per_owner, per_owner)]
            place = target.at[pl.ds(c * per_owner, per_owner)]
            copies.append(pltpu.make_async_copy(part, place, sems.at[i * columns + c]))
    for copy in copies:
        copy.start()
    return copies


def pack_kernel(info, gate_rows, up_rows, gate, up, down, rows_out, both_out, down_out, sems):
    count = down_out.shape[0]
    targets = both_out.at[pl.ds(0, count)], both_out.at[pl.ds(count, count)], down_out
    copies = copy_owner(zip((gate, up, down), targets), info[OWNER], sems)
    columns, per_owner = rows_out.shape[1:]
    for i, rows in enumerate((gate_rows, up_rows)):
        for c in range(columns):
            for k in range(per_owner):
                rows_out[i, c, k] = rows[c, info[OWNER] * per_owner + k] - info[OWNER] * info[OWNED]
    for copy in copies:
        copy.wait()


def scatter_rows(dense, packed, rows, i):
    columns, per_owner = rows.shape[1:]
    size = packed.shape[1]
    dense[...] = jnp.zeros_like(dense)
    for c in range(columns):
        for k in range(per_owner):
            place = pl.ds(aligned(rows[i, c, k], size), size)
            dense[place, c * size : (c + 1) * size] = packed[(i * columns + c) * per_owner + k]


def project_kernel(n, i, info, rows, *refs):
    xs, packed = refs[:n], refs[n]
    near, far, dense, total = refs[n + 1 :]
    scatter_rows(dense, packed, rows, i)
    for r, x in enumerate(xs):
        total[r] = jnp.dot(x[...], dense[...], preferred_element_type=F32)
        split_rows(total, r, near, far, info[Z])


def hidden_grad_kernel(nj, columns, info, down_rows, *refs):
    cots, down_blocks = refs[:nj], refs[nj]
    near, far, down_dense, total = refs[nj + 1 :]
    place = down_places(info, down_rows, columns, down_blocks.shape[0] // columns)
    scatter_cols(down_dense, down_blocks, place, columns)
    for r in range(nj):
        total[r] = lax.dot_general(
            cots[r][...], down_dense[...], (((1,), (1,)), ((), ())), preferred_element_type=F32
        )
        split_rows(total, r, near, far, info[Z])


def own_place(dx, d):
    return dx ^ (d & 1)


def add_kernel(n_dp, n_tok, bit, near, arrived, near_out, far_out):
    for d in range(near.shape[0]):
        out = far_out if d % 2 else near_out
        for dx in range(n_dp):
            there = pl.ds(own_place(dx, bit) * n_tok, n_tok)
            here = pl.ds(dx * n_tok, n_tok)
            out[d // 2, here] = (near[d, here] + arrived[d, there].astype(F32)).astype(out.dtype)


def hidden_kernel(gate_near, gate_last, up_near, up_last, sums, hidden):
    gate = gate_near[0] + gate_last[0].astype(F32)
    up = up_near[0] + up_last[0].astype(F32)
    sums[0] = gate
    sums[1] = up
    hidden[...] = (gate * jax.nn.sigmoid(gate) * up).astype(BF)


def act_grad_kernel(sums, near, last, gate_act, up_act):
    hidden_grad = near[0] + last[0].astype(F32)
    gate, up = sums[0], sums[1]
    s = jax.nn.sigmoid(gate)
    gate_act[...] = (hidden_grad * up * s * (1.0 + gate * (1.0 - s))).astype(BF)
    up_act[...] = (hidden_grad * (gate * s)).astype(BF)


def join_rows(joined, parts, z, n_tok):
    rows = parts[0].shape[1]
    for r in range(joined.shape[0]):
        dx, dc = divmod(r, n_tok)
        for d, part in enumerate(parts):
            joined[r, pl.ds(aligned(z ^ d, rows), rows), :] = part[own_place(dx, d) * n_tok + dc]


def weight_grad(acc, left, rights, stage, sems):
    copies = [pltpu.make_async_copy(right, stage.at[r], sems.at[r]) for r, right in enumerate(rights)]
    for copy in copies:
        copy.start()
    for r, copy in enumerate(copies):
        copy.wait()
        term = lax.dot_general(left[r], stage[r], (((0,), (0,)), ((), ())), preferred_element_type=F32)
        if r == 0:
            acc[...] = term
        else:
            acc[...] += term


def pick_blocks(out, acc, place, transposed):
    columns, per_owner, size, _ = out.shape
    for c in range(columns):
        for k in range(per_owner):
            block = acc[c * size : (c + 1) * size, pl.ds(aligned(place(c, k), size), size)]
            out[c, k] = (block.T if transposed else block).astype(BF)


def put_plane(keep, send, r, n_tok, value):
    dx, dc = divmod(r, n_tok)
    if dc == 0:
        keep[dx][...] = value
    else:
        send[dx][dc - 1] = value.astype(BF)


def sum_kernel(first, *refs):
    *others, out = refs
    total = first[...]
    for other in others:
        value = other[...].astype(F32)
        total += value if value.ndim == total.ndim else jnp.sum(value, axis=0)
    out[...] = total.astype(BF)


def deliver_kernel(*refs):
    count = len(refs) // 2
    for source, out in zip(refs[:count], refs[count:]):
        out[...] = source[...]


def mixed_kernel(shards, n_dp, n_tok, info, *refs):
    hiddens, dense = refs[:shards], refs[shards]
    keep, send = refs[shards + 1 : shards + 1 + n_dp], refs[shards + 1 + n_dp : shards + 1 + 2 * n_dp]
    joined = refs[shards + 1 + 2 * n_dp]
    join_rows(joined, hiddens, info[Z], n_tok)
    for r in reversed(range(joined.shape[0])):
        put_plane(keep, send, r, n_tok, jnp.dot(joined[r], dense[...], preferred_element_type=F32))


def down_grad_kernel(info, down_rows, joined, *refs):
    *rights, grad, acc, stage, sems = refs
    weight_grad(acc, joined, rights, stage, sems)
    pick_blocks(grad, acc, down_places(info, down_rows, *grad.shape[:2]), False)


def up_grad_kernel(rows, joined, *refs):
    *rights, grad, acc, stage, sems = refs
    weight_grad(acc, joined, rights, stage, sems)
    pick_blocks(grad, acc, lambda c, k: rows[1, c, k], True)


def gate_grad_kernel(shards, nj, n_tok, info, rows, *refs):
    acts = refs[:shards]
    xs = refs[shards : shards + nj]
    grad, joined, acc, stage, sems = refs[shards + nj :]
    join_rows(joined, acts, info[Z], n_tok)
    weight_grad(acc, joined, xs, stage, sems)
    pick_blocks(grad, acc, lambda c, k: rows[0, c, k], True)


def tokens_grad_kernel(shards, n_dp, n_tok, info, *refs):
    acts = refs[:shards]
    joined_gate, gate_dense, up_dense = refs[shards : shards + 3]
    keep, send = refs[shards + 3 : shards + 3 + n_dp], refs[shards + 3 + n_dp : shards + 3 + 2 * n_dp]
    joined = refs[shards + 3 + 2 * n_dp]
    join_rows(joined, acts, info[Z], n_tok)
    contract = (((1,), (1,)), ((), ()))
    for r in reversed(range(joined.shape[0])):
        value = lax.dot_general(joined_gate[r], gate_dense[...], contract, preferred_element_type=F32)
        value += lax.dot_general(joined[r], up_dense[...], contract, preferred_element_type=F32)
        put_plane(keep, send, r, n_tok, value)


def shape(dims, dtype):
    return jax.ShapeDtypeStruct(dims, dtype)


def body(n_dp, n_tok, shards, tokens, gate_blocks, up_blocks, down_blocks, gate_rows, up_rows, down_rows, cotangent):
    nj = n_dp * n_tok
    z = lax.axis_index("shard")
    x_index, c_index = lax.axis_index("dp"), lax.axis_index("tok")
    q = column_shard(n_dp, z, x_index, c_index)
    count, width = tokens.shape
    columns, nonzero, size, _ = gate_blocks.shape
    per_owner = nonzero // shards
    owned = width // size
    hidden_width = columns * size
    part = count // shards
    blocks = columns * per_owner

    def reduce(near, far):
        bit = 1
        while bit < shards:
            arrived = lax.ppermute(far, ("shard", "dp"), shard_perm(shards, n_dp, bit))
            if near.shape[0] == 1:
                return near, arrived
            half = (near.shape[0] // 2, *near.shape[1:])
            near, far = run(
                functools.partial(add_kernel, n_dp, n_tok, bit), [], [near, arrived], [shape(half, F32), shape(half, BF)], [], 0
            )
            bit *= 2

    def gather(own):
        have = {0: own}
        bit = shards // 2
        while bit:
            for d in sorted(have):
                have[d ^ bit] = lax.ppermute(have[d], ("shard", "dp"), shard_perm(shards, n_dp, bit))
            bit //= 2
        return [have[d] for d in range(shards)]

    def run(kernel, scalars, arrays, outs, scratch, flops, kept=(), limit=LIMIT, out_spaces=None):
        return call(kernel, scalars, arrays, outs, scratch, flops, kept, limit, out_spaces)

    def gather_plane(own):
        got = []
        for dx in range(n_dp):
            base = own if dx == 0 else lax.ppermute(own, "dp", xor_perm(n_dp, dx))
            got.append(base)
            for dc in range(1, n_tok):
                got.append(lax.ppermute(base, "tok", xor_perm(n_tok, dc)))
        return got

    w_perm = weight_perm(shards, n_dp, n_tok)
    owner = weight_owner(shards, n_dp, n_tok, z, x_index, c_index)
    info = jnp.stack([v.astype(jnp.int32) for v in (z, q, owner, jnp.int32(owned))])
    rows, both_parts, down_part = run(
        pack_kernel,
        [info, gate_rows, up_rows],
        [],
        [shape((2, columns, per_owner), jnp.int32)] + [shape((n * blocks, size, size), BF) for n in (2, 1)],
        [pltpu.SemaphoreType.DMA((3 * columns,))],
        0,
        [gate_blocks, up_blocks, down_blocks],
        60 << 20,
        [pltpu.SMEM] + [pltpu.VMEM] * 2,
    )
    both_parts = lax.ppermute(both_parts, PLANE, w_perm)
    rows = lax.ppermute(rows, PLANE, w_perm)
    down_part = lax.ppermute(down_part, PLANE, w_perm)

    xs = gather_plane(tokens)
    cots = gather_plane(cotangent)
    macs = nj * count * width * hidden_width * 2
    joined = pltpu.VMEM((nj, count, hidden_width), BF)
    joined_shape = shape((nj, count, hidden_width), BF)
    acc = pltpu.VMEM((hidden_width, width), F32)
    dense = shape((width, hidden_width), BF)

    parts = (shards // 2, nj, part, hidden_width)
    part_shapes = [shape(parts, F32), shape(parts, BF)]

    sums_scratch = [pltpu.VMEM((nj, count, hidden_width), F32)]

    def project(i):
        return run(
            functools.partial(project_kernel, nj, i),
            [info, rows],
            [*xs, both_parts],
            part_shapes + [dense],
            sums_scratch,
            macs,
        )

    near_gate, far_gate, gate_dense = project(0)
    gates = reduce(near_gate, far_gate)
    near_up, far_up, up_dense = project(1)
    ups = reduce(near_up, far_up)
    near_hg, far_hg, down_dense = run(
        functools.partial(hidden_grad_kernel, nj, columns),
        [info, down_rows],
        [*cots, down_part],
        part_shapes + [shape((hidden_width, width), BF)],
        sums_scratch,
        macs,
    )
    hidden_grads = reduce(near_hg, far_hg)
    act = shape((nj, part, hidden_width), BF)
    sums, hidden = run(
        hidden_kernel, [], [*gates, *ups], [shape((2, nj, part, hidden_width), F32), act], [], macs // 64
    )
    hiddens = gather(hidden)
    gate_act, up_act = run(act_grad_kernel, [], [sums, *hidden_grads], [act, act], [], macs // 64)
    gate_acts = gather(gate_act)
    up_acts = gather(up_act)

    plane_shapes = [shape((count, width), F32)] * n_dp + [shape((n_tok - 1, count, width), BF)] * n_dp
    grad_shape = shape((columns, per_owner, size, size), BF)
    *mixed, joined_hidden = run(
        functools.partial(mixed_kernel, shards, n_dp, n_tok),
        [info],
        [*hiddens, down_dense],
        plane_shapes + [joined_shape],
        [],
        macs,
    )
    staged = [acc, pltpu.VMEM((nj, count, width), BF), pltpu.SemaphoreType.DMA((nj,))]
    (down_grad,) = run(down_grad_kernel, [info, down_rows], [joined_hidden], [grad_shape], staged, macs, cots)
    gate_grad, joined_gate = run(
        functools.partial(gate_grad_kernel, shards, nj, n_tok),
        [info, rows],
        gate_acts,
        [grad_shape, joined_shape],
        staged,
        macs,
        xs,
    )
    *tokens_terms, joined_up = run(
        functools.partial(tokens_grad_kernel, shards, n_dp, n_tok),
        [info],
        [*up_acts, joined_gate, gate_dense, up_dense],
        plane_shapes + [joined_shape],
        [],
        2 * macs,
    )
    (up_grad,) = run(up_grad_kernel, [rows], [joined_up], [grad_shape], staged, macs, xs)

    def sum_plane(terms):
        arrived = []
        total = lambda parts: run(sum_kernel, [], parts, [shape((count, width), BF)], [], 0)[0]
        for dx in reversed(range(n_dp)):
            parts = [terms[dx]]
            if n_tok == 2:
                parts.append(lax.ppermute(terms[n_dp + dx], "tok", xor_perm(n_tok, 1)))
            else:
                for dc in range(1, n_tok):
                    parts.append(lax.ppermute(terms[n_dp + dx][dc - 1], "tok", xor_perm(n_tok, dc)))
            if dx:
                arrived.append(lax.ppermute(total(parts), "dp", xor_perm(n_dp, dx)))
        return total(parts + arrived)

    g_perm = grad_perm(shards, n_dp, n_tok)

    def home(grad):
        grad = lax.ppermute(grad, PLANE, g_perm)
        return run(deliver_kernel, [], [grad], [grad_shape], [], 0)[0]

    return (sum_plane(mixed), sum_plane(tokens_terms), home(gate_grad), home(up_grad), home(down_grad))


def solution(mesh):
    shards, n_dp, n_tok = (mesh.shape[name] for name in PLANE)
    assert shards == n_dp * n_tok
    in_specs = (
        P(("groups", "dp", "tok"), "shard"),
        P("shard", None, None, None),
        P("shard", None, None, None),
        P("shard", None, None, None),
        P("shard", None),
        P("shard", None),
        P(),
        P(("groups", "dp", "tok"), "shard"),
    )
    out_specs = (
        P(("groups", "dp", "tok"), "shard"),
        P(("groups", "dp", "tok"), "shard"),
        P(("groups", "shard"), ("dp", "tok"), None, None),
        P(("groups", "shard"), ("dp", "tok"), None, None),
        P(("groups", "shard"), ("dp", "tok"), None, None),
    )
    program = functools.partial(body, n_dp, n_tok, shards)
    return jax.shard_map(program, mesh=mesh, in_specs=in_specs, out_specs=out_specs, check_vma=False)
```

```python
import functools

import jax
import jax.numpy as jnp
from jax import lax
from jax.experimental import pallas as pl
from jax.experimental.pallas import tpu as pltpu
from jax.sharding import PartitionSpec as P

BF = jnp.bfloat16
F32 = jnp.float32
LIMIT = 16 << 20
Z, Q, OWNER, OWNED = range(4)
PLANE = ("shard", "dp", "tok")


def xor_perm(count, step):
    return [(i, i ^ step) for i in range(count)]


def column_shard(n_dp, z, x, c):
    return c * n_dp + (x ^ (z & 1))


def shard_perm(shards, n_dp, d):
    return [(z * n_dp + x, (z ^ d) * n_dp + (x ^ (d & 1))) for z in range(shards) for x in range(n_dp)]


def weight_perm(shards, n_dp, n_tok):
    pairs = []
    for z in range(shards):
        for x in range(n_dp):
            for c in range(n_tok):
                source = x * n_tok + z // 2 if (shards, n_dp, n_tok) == (4, 2, 2) else z
                plane = column_shard(n_dp, z, x, c) * n_dp * n_tok
                pairs.append((plane + source, (z * n_dp + x) * n_tok + c))
    return pairs


def weight_owner(shards, n_dp, n_tok, z, x, c):
    if (shards, n_dp, n_tok) == (4, 2, 2):
        return c * 2 + (x ^ (z & 1))
    return x * n_tok + c


def grad_perm(shards, n_dp, n_tok):
    return [
        ((z * n_dp + x) * n_tok + c, column_shard(n_dp, z, x, c) * n_dp * n_tok + z)
        for z in range(shards)
        for x in range(n_dp)
        for c in range(n_tok)
    ]


def vmem(count):
    return [pl.BlockSpec(memory_space=pltpu.VMEM)] * count


def smem(count):
    return [pl.BlockSpec(memory_space=pltpu.SMEM)] * count


def call(kernel, scalars, arrays, outs, scratch, flops, kept, limit, out_spaces):
    moved = sum(a.size * a.dtype.itemsize for a in (*arrays, *kept))
    moved += sum(o.size * o.dtype.itemsize for o in outs)
    return pl.pallas_call(
        kernel,
        out_shape=outs,
        in_specs=smem(len(scalars)) + vmem(len(arrays)) + [pl.BlockSpec(memory_space=pltpu.HBM)] * len(kept),
        out_specs=[pl.BlockSpec(memory_space=s) for s in out_spaces] if out_spaces else vmem(len(outs)),
        scratch_shapes=scratch,
        compiler_params=pltpu.CompilerParams(vmem_limit_bytes=limit),
        cost_estimate=pl.CostEstimate(flops=flops, bytes_accessed=moved, transcendentals=0),
    )(*scalars, *arrays, *kept)


def aligned(value, size):
    return pl.multiple_of(value * size, size)


def down_places(info, down_rows, columns, per_owner, dx=0):
    first_row, first = (info[Q] ^ dx) * columns, info[Z] * per_owner
    return lambda c, k: down_rows[first_row + c, first + k] - info[Z] * info[OWNED]


def scatter_cols(dense, packed, place, columns):
    count, size, _ = packed.shape
    per_owner = count // columns
    dense[...] = jnp.zeros_like(dense)
    for c in range(columns):
        for k in range(per_owner):
            here = pl.ds(aligned(place(c, k), size), size)
            dense[c * size : (c + 1) * size, here] = packed[c * per_owner + k]


def split_rows(total, r, near, far, z):
    rows = near.shape[2]
    for d in range(2 * near.shape[0]):
        out = far if d % 2 else near
        out[d // 2, r] = total[r, pl.ds(aligned(z ^ d, rows), rows), :].astype(out.dtype)


def copy_owner(pairs, owner, sems):
    copies = []
    for i, (source, target) in enumerate(pairs):
        columns = source.shape[0]
        per_owner = target.shape[0] // columns
        for c in range(columns):
            part = source.at[c, pl.ds(owner * per_owner, per_owner)]
            place = target.at[pl.ds(c * per_owner, per_owner)]
            copies.append(pltpu.make_async_copy(part, place, sems.at[i * columns + c]))
    for copy in copies:
        copy.start()
    return copies


def pack_kernel(info, gate_rows, up_rows, gate, up, down, rows_out, both_out, down_out, sems):
    count = down_out.shape[0]
    targets = both_out.at[pl.ds(0, count)], both_out.at[pl.ds(count, count)], down_out
    copies = copy_owner(zip((gate, up, down), targets), info[OWNER], sems)
    columns, per_owner = rows_out.shape[1:]
    for i, rows in enumerate((gate_rows, up_rows)):
        for c in range(columns):
            for k in range(per_owner):
                rows_out[i, c, k] = rows[c, info[OWNER] * per_owner + k] - info[OWNER] * info[OWNED]
    for copy in copies:
        copy.wait()


def scatter_rows(dense, packed, rows, i):
    columns, per_owner = rows.shape[1:]
    size = packed.shape[1]
    dense[...] = jnp.zeros_like(dense)
    for c in range(columns):
        for k in range(per_owner):
            place = pl.ds(aligned(rows[i, c, k], size), size)
            dense[place, c * size : (c + 1) * size] = packed[(i * columns + c) * per_owner + k]


def project_kernel(n, i, info, rows, *refs):
    xs, packed = refs[:n], refs[n]
    near, far, dense, total = refs[n + 1 :]
    scatter_rows(dense, packed, rows, i)
    for r, x in enumerate(xs):
        total[r] = jnp.dot(x[...], dense[...], preferred_element_type=F32)
        split_rows(total, r, near, far, info[Z])


def hidden_grad_kernel(nj, columns, info, down_rows, *refs):
    cots, down_blocks = refs[:nj], refs[nj]
    near, far, down_dense, total = refs[nj + 1 :]
    place = down_places(info, down_rows, columns, down_blocks.shape[0] // columns)
    scatter_cols(down_dense, down_blocks, place, columns)
    for r in range(nj):
        total[r] = lax.dot_general(
            cots[r][...], down_dense[...], (((1,), (1,)), ((), ())), preferred_element_type=F32
        )
        split_rows(total, r, near, far, info[Z])


def own_place(dx, d):
    return dx ^ (d & 1)


def add_kernel(n_dp, n_tok, bit, near, arrived, near_out, far_out):
    for d in range(near.shape[0]):
        out = far_out if d % 2 else near_out
        for dx in range(n_dp):
            there = pl.ds(own_place(dx, bit) * n_tok, n_tok)
            here = pl.ds(dx * n_tok, n_tok)
            out[d // 2, here] = (near[d, here] + arrived[d, there].astype(F32)).astype(out.dtype)


def hidden_kernel(gate_near, gate_last, up_near, up_last, sums, hidden):
    gate = gate_near[0] + gate_last[0].astype(F32)
    up = up_near[0] + up_last[0].astype(F32)
    sums[0] = gate
    sums[1] = up
    hidden[...] = (gate * jax.nn.sigmoid(gate) * up).astype(BF)


def act_grad_kernel(sums, near, last, gate_act, up_act):
    hidden_grad = near[0] + last[0].astype(F32)
    gate, up = sums[0], sums[1]
    s = jax.nn.sigmoid(gate)
    gate_act[...] = (hidden_grad * up * s * (1.0 + gate * (1.0 - s))).astype(BF)
    up_act[...] = (hidden_grad * (gate * s)).astype(BF)


def join_kernel(shards, n_dp, n_tok, info, *refs):
    parts, joined = refs[:shards], refs[shards:]
    rows = parts[0].shape[1]
    for dx in range(n_dp):
        for dc in range(n_tok):
            for d, part in enumerate(parts):
                here = pl.ds(aligned(info[Z] ^ d, rows), rows)
                joined[dx][dc, here, :] = part[own_place(dx, d) * n_tok + dc]


def weight_grad(acc, lefts, rights, stage, sems):
    copies = [pltpu.make_async_copy(right, stage.at[r], sems.at[r]) for r, right in enumerate(rights)]
    for copy in copies:
        copy.start()
    n_tok = lefts[0].shape[0]
    for r, copy in enumerate(copies):
        copy.wait()
        left = lefts[r // n_tok][r % n_tok]
        term = lax.dot_general(left, stage[r], (((0,), (0,)), ((), ())), preferred_element_type=F32)
        if r == 0:
            acc[...] = term
        else:
            acc[...] += term


def pick_blocks(out, acc, place, transposed):
    columns, per_owner, size, _ = out.shape
    for c in range(columns):
        for k in range(per_owner):
            block = acc[c * size : (c + 1) * size, pl.ds(aligned(place(c, k), size), size)]
            out[c, k] = (block.T if transposed else block).astype(BF)


def sum_kernel(first, *refs):
    *others, out = refs
    total = first[...]
    for other in others:
        value = other[...].astype(F32)
        total += value if value.ndim == total.ndim else jnp.sum(value, axis=0)
    out[...] = total.astype(BF)


def deliver_kernel(*refs):
    count = len(refs) // 2
    for source, out in zip(refs[:count], refs[count:]):
        out[...] = source[...]


def put_plane(keep, send, dc, value):
    if dc == 0:
        keep[...] = value
    else:
        send[dc - 1] = value.astype(BF)


def mixed_kernel(n_dp, columns, info, down_rows, *refs):
    hiddens, dense = refs[:n_dp], refs[n_dp]
    others = refs[n_dp + 1 : 2 * n_dp]
    keep, send = refs[2 * n_dp : 2 * n_dp + 2]
    denses = [dense, *refs[2 * n_dp + 2 :]]
    for dx in range(1, n_dp):
        packed = others[dx - 1]
        place = down_places(info, down_rows, columns, packed.shape[0] // columns, dx)
        scatter_cols(denses[dx], packed, place, columns)
    for dc in reversed(range(hiddens[0].shape[0])):
        value = 0.0
        for hidden, weights in zip(hiddens, denses):
            value += jnp.dot(hidden[dc], weights[...], preferred_element_type=F32)
        put_plane(keep, send, dc, value)


def down_grad_kernel(n_dp, info, down_rows, *refs):
    lefts = refs[:n_dp]
    *rights, grad, acc, stage, sems = refs[n_dp:]
    weight_grad(acc, lefts, rights, stage, sems)
    pick_blocks(grad, acc, down_places(info, down_rows, *grad.shape[:2]), False)


def row_grad_kernel(n_dp, i, rows, *refs):
    lefts = refs[:n_dp]
    *rights, grad, acc, stage, sems = refs[n_dp:]
    weight_grad(acc, lefts, rights, stage, sems)
    pick_blocks(grad, acc, lambda c, k: rows[i, c, k], True)


def tokens_grad_kernel(n_dp, *refs):
    other_rows = refs[: n_dp - 1]
    refs = refs[n_dp - 1 :]
    sides = refs[:n_dp], refs[n_dp : 2 * n_dp]
    gate_dense, up_dense = refs[2 * n_dp : 2 * n_dp + 2]
    others = refs[2 * n_dp + 2 : 3 * n_dp + 1]
    keep, send = refs[3 * n_dp + 1 : 3 * n_dp + 3]
    scratch = refs[3 * n_dp + 3 :]
    denses = [gate_dense, *scratch[: n_dp - 1]], [up_dense, *scratch[n_dp - 1 :]]
    for i, side in enumerate(denses):
        for packed, rows, dense in zip(others, other_rows, side[1:]):
            scatter_rows(dense, packed, rows, i)
    for dc in reversed(range(sides[0][0].shape[0])):
        value = 0.0
        for acts, side in zip(sides, denses):
            for act, weights in zip(acts, side):
                value += lax.dot_general(act[dc], weights[...], (((1,), (1,)), ((), ())), preferred_element_type=F32)
        put_plane(keep, send, dc, value)


def shape(dims, dtype):
    return jax.ShapeDtypeStruct(dims, dtype)


def body(n_dp, n_tok, shards, tokens, gate_blocks, up_blocks, down_blocks, gate_rows, up_rows, down_rows, cotangent):
    nj = n_dp * n_tok
    z = lax.axis_index("shard")
    x_index, c_index = lax.axis_index("dp"), lax.axis_index("tok")
    q = column_shard(n_dp, z, x_index, c_index)
    count, width = tokens.shape
    columns, nonzero, size, _ = gate_blocks.shape
    per_owner = nonzero // shards
    owned = width // size
    hidden_width = columns * size
    part = count // shards
    blocks = columns * per_owner

    def reduce(near, far):
        bit = 1
        while bit < shards:
            arrived = lax.ppermute(far, ("shard", "dp"), shard_perm(shards, n_dp, bit))
            if near.shape[0] == 1:
                return near, arrived
            half = (near.shape[0] // 2, *near.shape[1:])
            near, far = run(
                functools.partial(add_kernel, n_dp, n_tok, bit), [], [near, arrived], [shape(half, F32), shape(half, BF)], [], 0
            )
            bit *= 2

    def gather(own):
        have = {0: own}
        bit = shards // 2
        while bit:
            for d in sorted(have):
                have[d ^ bit] = lax.ppermute(have[d], ("shard", "dp"), shard_perm(shards, n_dp, bit))
            bit //= 2
        return [have[d] for d in range(shards)]

    def run(kernel, scalars, arrays, outs, scratch, flops, kept=(), limit=LIMIT, out_spaces=None):
        return call(kernel, scalars, arrays, outs, scratch, flops, kept, limit, out_spaces)

    def gather_plane(own):
        got = []
        for dx in range(n_dp):
            base = own if dx == 0 else lax.ppermute(own, "dp", xor_perm(n_dp, dx))
            got.append(base)
            for dc in range(1, n_tok):
                got.append(lax.ppermute(base, "tok", xor_perm(n_tok, dc)))
        return got

    w_perm = weight_perm(shards, n_dp, n_tok)
    owner = weight_owner(shards, n_dp, n_tok, z, x_index, c_index)
    info = jnp.stack([v.astype(jnp.int32) for v in (z, q, owner, jnp.int32(owned))])
    rows, both_parts, down_part = run(
        pack_kernel,
        [info, gate_rows, up_rows],
        [],
        [shape((2, columns, per_owner), jnp.int32)] + [shape((n * blocks, size, size), BF) for n in (2, 1)],
        [pltpu.SemaphoreType.DMA((3 * columns,))],
        0,
        [gate_blocks, up_blocks, down_blocks],
        60 << 20,
        [pltpu.SMEM] + [pltpu.VMEM] * 2,
    )
    both_parts = lax.ppermute(both_parts, PLANE, w_perm)
    rows = lax.ppermute(rows, PLANE, w_perm)
    down_part = lax.ppermute(down_part, PLANE, w_perm)

    xs = gather_plane(tokens)
    cots = gather_plane(cotangent)
    macs = nj * count * width * hidden_width * 2
    acc = pltpu.VMEM((hidden_width, width), F32)
    dense = shape((width, hidden_width), BF)

    parts = (shards // 2, nj, part, hidden_width)
    part_shapes = [shape(parts, F32), shape(parts, BF)]

    sums_scratch = [pltpu.VMEM((nj, count, hidden_width), F32)]

    def project(i):
        return run(
            functools.partial(project_kernel, nj, i),
            [info, rows],
            [*xs, both_parts],
            part_shapes + [dense],
            sums_scratch,
            macs,
        )

    near_gate, far_gate, gate_dense = project(0)
    gates = reduce(near_gate, far_gate)
    near_up, far_up, up_dense = project(1)
    ups = reduce(near_up, far_up)
    near_hg, far_hg, down_dense = run(
        functools.partial(hidden_grad_kernel, nj, columns),
        [info, down_rows],
        [*cots, down_part],
        part_shapes + [shape((hidden_width, width), BF)],
        sums_scratch,
        macs,
    )
    near_hg, last_hg = reduce(near_hg, far_hg)
    act = shape((nj, part, hidden_width), BF)
    sums, hidden = run(
        hidden_kernel, [], [*gates, *ups], [shape((2, nj, part, hidden_width), F32), act], [], macs // 64
    )
    gate_act, up_act = run(act_grad_kernel, [], [sums, near_hg, last_hg], [act, act], [], macs // 64)

    chip = shape((n_tok, count, hidden_width), BF)
    others = range(1, n_dp)
    to_dp = lambda a, dx: lax.ppermute(a, "dp", xor_perm(n_dp, dx))
    other_both = [to_dp(both_parts, dx) for dx in others]
    other_rows = [to_dp(rows, dx) for dx in others]
    other_down = [to_dp(down_part, dx) for dx in others]

    def join(own):
        parts = gather(own)
        joined = run(functools.partial(join_kernel, shards, n_dp, n_tok), [info], parts, [chip] * n_dp, [], 0)
        return joined, [joined[0]] + [to_dp(joined[dx], dx) for dx in others]

    all_hidden, chip_hidden = join(hidden)
    all_gate, chip_gate = join(gate_act)
    all_up, chip_up = join(up_act)

    plane_shapes = [shape((count, width), F32), shape((n_tok - 1, count, width), BF)]
    grad_shape = shape((columns, per_owner, size, size), BF)
    staged = [acc, pltpu.VMEM((nj, count, width), BF), pltpu.SemaphoreType.DMA((nj,))]
    mixed = run(
        functools.partial(mixed_kernel, n_dp, columns),
        [info, down_rows],
        [*chip_hidden, down_dense, *other_down],
        plane_shapes,
        [pltpu.VMEM((hidden_width, width), BF)] * (n_dp - 1),
        macs,
    )
    (down_grad,) = run(
        functools.partial(down_grad_kernel, n_dp), [info, down_rows], all_hidden, [grad_shape], staged, macs, cots
    )

    def row_grad(i, lefts):
        kernel = functools.partial(row_grad_kernel, n_dp, i)
        return run(kernel, [rows], lefts, [grad_shape], staged, macs, xs)[0]

    gate_grad = row_grad(0, all_gate)
    up_grad = row_grad(1, all_up)
    tokens_terms = run(
        functools.partial(tokens_grad_kernel, n_dp),
        other_rows,
        [*chip_gate, *chip_up, gate_dense, up_dense, *other_both],
        plane_shapes,
        [pltpu.VMEM((width, hidden_width), BF)] * (2 * n_dp - 2),
        2 * macs,
    )

    def sum_plane(terms):
        keep, send = terms
        if n_tok == 2:
            arrived = [lax.ppermute(send, "tok", xor_perm(n_tok, 1))]
        else:
            arrived = [lax.ppermute(send[dc - 1], "tok", xor_perm(n_tok, dc)) for dc in range(1, n_tok)]
        return run(sum_kernel, [], [keep, *arrived], [shape((count, width), BF)], [], 0)[0]

    g_perm = grad_perm(shards, n_dp, n_tok)

    def home(grad):
        grad = lax.ppermute(grad, PLANE, g_perm)
        return run(deliver_kernel, [], [grad], [grad_shape], [], 0)[0]

    return (sum_plane(mixed), sum_plane(tokens_terms), home(gate_grad), home(up_grad), home(down_grad))


def solution(mesh):
    shards, n_dp, n_tok = (mesh.shape[name] for name in PLANE)
    assert shards == n_dp * n_tok
    in_specs = (
        P(("groups", "dp", "tok"), "shard"),
        P("shard", None, None, None),
        P("shard", None, None, None),
        P("shard", None, None, None),
        P("shard", None),
        P("shard", None),
        P(),
        P(("groups", "dp", "tok"), "shard"),
    )
    out_specs = (
        P(("groups", "dp", "tok"), "shard"),
        P(("groups", "dp", "tok"), "shard"),
        P(("groups", "shard"), ("dp", "tok"), None, None),
        P(("groups", "shard"), ("dp", "tok"), None, None),
        P(("groups", "shard"), ("dp", "tok"), None, None),
    )
    program = functools.partial(body, n_dp, n_tok, shards)
    return jax.shard_map(program, mesh=mesh, in_specs=in_specs, out_specs=out_specs, check_vma=False)
```

```python
import functools

import jax
import jax.numpy as jnp
from jax import lax
from jax.experimental import pallas as pl
from jax.experimental.pallas import tpu as pltpu
from jax.sharding import PartitionSpec as P

BF = jnp.bfloat16
F32 = jnp.float32
LIMIT = 16 << 20
Z, Q, OWNER, OWNED, GROUP = range(5)
PLANE = ("shard", "dp", "tok")


def xor_perm(count, step):
    return [(i, i ^ step) for i in range(count)]


def column_shard(n_dp, z, x, c):
    return c * n_dp + (x ^ (z & 1))


def shard_perm(shards, n_dp, d):
    return [(z * n_dp + x, (z ^ d) * n_dp + (x ^ (d & 1))) for z in range(shards) for x in range(n_dp)]


def weight_perm(shards, n_dp, n_tok):
    pairs = []
    for z in range(shards):
        for x in range(n_dp):
            for c in range(n_tok):
                source = x * n_tok + z // 2 if (shards, n_dp, n_tok) == (4, 2, 2) else z
                plane = column_shard(n_dp, z, x, c) * n_dp * n_tok
                pairs.append((plane + source, (z * n_dp + x) * n_tok + c))
    return pairs


def weight_owner(shards, n_dp, n_tok, z, x, c):
    if (shards, n_dp, n_tok) == (4, 2, 2):
        return c * 2 + (x ^ (z & 1))
    return x * n_tok + c


def grad_perm(shards, n_dp, n_tok):
    return [
        ((z * n_dp + x) * n_tok + c, column_shard(n_dp, z, x, c) * n_dp * n_tok + z)
        for z in range(shards)
        for x in range(n_dp)
        for c in range(n_tok)
    ]


def vmem(count):
    return [pl.BlockSpec(memory_space=pltpu.VMEM)] * count


def smem(count):
    return [pl.BlockSpec(memory_space=pltpu.SMEM)] * count


def call(kernel, scalars, arrays, outs, scratch, flops, kept, limit, out_spaces):
    moved = sum(a.size * a.dtype.itemsize for a in (*arrays, *kept))
    moved += sum(o.size * o.dtype.itemsize for o in outs)
    return pl.pallas_call(
        kernel,
        out_shape=outs,
        in_specs=smem(len(scalars)) + vmem(len(arrays)) + [pl.BlockSpec(memory_space=pltpu.HBM)] * len(kept),
        out_specs=[pl.BlockSpec(memory_space=s) for s in out_spaces] if out_spaces else vmem(len(outs)),
        scratch_shapes=scratch,
        compiler_params=pltpu.CompilerParams(vmem_limit_bytes=limit),
        cost_estimate=pl.CostEstimate(flops=flops, bytes_accessed=moved, transcendentals=0),
    )(*scalars, *arrays, *kept)


def aligned(value, size):
    return value * size if isinstance(value, int) else pl.multiple_of(value * size, size)


def down_places(info, down_rows, columns, per_owner, dx=0):
    first_row, first = (info[Q] ^ dx) * columns, info[Z] * per_owner
    return lambda c, k: down_rows[first_row + c, first + k] - info[Z] * info[OWNED]


def scatter_cols(dense, pieces, place):
    dense[...] = jnp.zeros_like(dense)
    for blocks, c in pieces:
        per_owner, size, _ = blocks.shape
        for k in range(per_owner):
            here = pl.ds(aligned(place(c, k), size), size)
            dense[pl.ds(aligned(c, size), size), here] = blocks[k]


def split_rows(total, r, near, far, z):
    rows = near.shape[2]
    for d in range(2 * near.shape[0]):
        out = far if d % 2 else near
        out[d // 2, r] = total[r, pl.ds(aligned(z ^ d, rows), rows), :].astype(out.dtype)


def pack_kernel(info, gate_rows, up_rows, gate, up, down, rows_out, gate_out, half_out, sems):
    columns, per_owner = rows_out.shape[1:]
    owner, group = info[OWNER], info[GROUP]
    here = pl.ds(owner * per_owner, per_owner)
    pairs = [(gate.at[c, here], gate_out.at[pl.ds(c * per_owner, per_owner)]) for c in range(columns)]
    pairs.append((up.at[group, here], half_out.at[pl.ds(0, per_owner)]))
    pairs.append((down.at[group, here], half_out.at[pl.ds(per_owner, per_owner)]))
    copies = [pltpu.make_async_copy(source, target, sems.at[n]) for n, (source, target) in enumerate(pairs)]
    for copy in copies:
        copy.start()
    for i, rows in enumerate((gate_rows, up_rows)):
        for c in range(columns):
            for k in range(per_owner):
                rows_out[i, c, k] = rows[c, owner * per_owner + k] - owner * info[OWNED]
    for copy in copies:
        copy.wait()


def gate_pieces(packed):
    per_owner = packed.shape[0] // 2
    return [(packed.at[pl.ds(c * per_owner, per_owner)], c) for c in range(2)]


def half_pieces(mine, other, group, i):
    per_owner = mine.shape[0] // 2
    here = pl.ds(i * per_owner, per_owner)
    return [(mine.at[here], group), (other.at[here], 1 - group)]


def scatter_rows(dense, pieces, rows, i):
    dense[...] = jnp.zeros_like(dense)
    for blocks, c in pieces:
        per_owner, size, _ = blocks.shape
        for k in range(per_owner):
            place = pl.ds(aligned(rows[i, c, k], size), size)
            dense[place, pl.ds(aligned(c, size), size)] = blocks[k]


def gate_kernel(n, info, rows, *refs):
    xs, packed = refs[:n], refs[n]
    near, far, dense, total = refs[n + 1 :]
    scatter_rows(dense, gate_pieces(packed), rows, 0)
    project(xs, near, far, dense, total, info[Z])


def up_kernel(n, info, rows, *refs):
    xs, (mine, other) = refs[:n], refs[n : n + 2]
    near, far, dense, total = refs[n + 2 :]
    scatter_rows(dense, half_pieces(mine, other, info[GROUP], 0), rows, 1)
    project(xs, near, far, dense, total, info[Z])


def project(xs, near, far, dense, total, z):
    for r, x in enumerate(xs):
        total[r] = jnp.dot(x[...], dense[...], preferred_element_type=F32)
        split_rows(total, r, near, far, z)


def hidden_grad_kernel(nj, columns, info, down_rows, *refs):
    cots, (mine, other) = refs[:nj], refs[nj : nj + 2]
    near, far, down_dense, total = refs[nj + 2 :]
    place = down_places(info, down_rows, columns, mine.shape[0] // 2)
    scatter_cols(down_dense, half_pieces(mine, other, info[GROUP], 1), place)
    for r in range(nj):
        total[r] = lax.dot_general(
            cots[r][...], down_dense[...], (((1,), (1,)), ((), ())), preferred_element_type=F32
        )
        split_rows(total, r, near, far, info[Z])


def own_place(dx, d):
    return dx ^ (d & 1)


def add_kernel(n_dp, n_tok, bit, near, arrived, near_out, far_out):
    for d in range(near.shape[0]):
        out = far_out if d % 2 else near_out
        for dx in range(n_dp):
            there = pl.ds(own_place(dx, bit) * n_tok, n_tok)
            here = pl.ds(dx * n_tok, n_tok)
            out[d // 2, here] = (near[d, here] + arrived[d, there].astype(F32)).astype(out.dtype)


def hidden_kernel(gate_near, gate_last, up_near, up_last, sums, hidden):
    gate = gate_near[0] + gate_last[0].astype(F32)
    up = up_near[0] + up_last[0].astype(F32)
    sums[0] = gate
    sums[1] = up
    hidden[...] = (gate * jax.nn.sigmoid(gate) * up).astype(BF)


def act_grad_kernel(sums, near, last, gate_act, up_act):
    hidden_grad = near[0] + last[0].astype(F32)
    gate, up = sums[0], sums[1]
    s = jax.nn.sigmoid(gate)
    gate_act[...] = (hidden_grad * up * s * (1.0 + gate * (1.0 - s))).astype(BF)
    up_act[...] = (hidden_grad * (gate * s)).astype(BF)


def join_kernel(shards, n_dp, n_tok, info, *refs):
    parts, joined = refs[:shards], refs[shards:]
    rows = parts[0].shape[1]
    for dx in range(n_dp):
        for dc in range(n_tok):
            for d, part in enumerate(parts):
                here = pl.ds(aligned(info[Z] ^ d, rows), rows)
                joined[dx][dc, here, :] = part[own_place(dx, d) * n_tok + dc]


def weight_grad(acc, lefts, rights, stage, sems):
    copies = [pltpu.make_async_copy(right, stage.at[r], sems.at[r]) for r, right in enumerate(rights)]
    for copy in copies:
        copy.start()
    n_tok = lefts[0].shape[0]
    for r, copy in enumerate(copies):
        copy.wait()
        left = lefts[r // n_tok][r % n_tok]
        term = lax.dot_general(left, stage[r], (((0,), (0,)), ((), ())), preferred_element_type=F32)
        if r == 0:
            acc[...] = term
        else:
            acc[...] += term


def pick_blocks(out, acc, place, transposed):
    columns, per_owner, size, _ = out.shape
    for c in range(columns):
        for k in range(per_owner):
            block = acc[c * size : (c + 1) * size, pl.ds(aligned(place(c, k), size), size)]
            out[c, k] = (block.T if transposed else block).astype(BF)


def sum_kernel(first, *refs):
    *others, out = refs
    total = first[...]
    for other in others:
        value = other[...].astype(F32)
        total += value if value.ndim == total.ndim else jnp.sum(value, axis=0)
    out[...] = total.astype(BF)


def deliver_kernel(*refs):
    count = len(refs) // 2
    for source, out in zip(refs[:count], refs[count:]):
        out[...] = source[...]


def put_plane(keep, send, dc, value):
    if dc == 0:
        keep[...] = value
    else:
        send[dc - 1] = value.astype(BF)


def mixed_kernel(n_dp, columns, info, down_rows, *refs):
    hiddens, dense = refs[:n_dp], refs[n_dp]
    halves = refs[n_dp + 1 : 3 * n_dp - 1]
    keep, send = refs[3 * n_dp - 1 : 3 * n_dp + 1]
    denses = [dense, *refs[3 * n_dp + 1 :]]
    for dx in range(1, n_dp):
        mine, other = halves[dx - 1], halves[n_dp + dx - 2]
        place = down_places(info, down_rows, columns, mine.shape[0] // 2, dx)
        scatter_cols(denses[dx], half_pieces(mine, other, info[GROUP], 1), place)
    for dc in reversed(range(hiddens[0].shape[0])):
        value = 0.0
        for hidden, weights in zip(hiddens, denses):
            value += jnp.dot(hidden[dc], weights[...], preferred_element_type=F32)
        put_plane(keep, send, dc, value)


def down_grad_kernel(n_dp, info, down_rows, *refs):
    lefts = refs[:n_dp]
    *rights, grad, acc, stage, sems = refs[n_dp:]
    weight_grad(acc, lefts, rights, stage, sems)
    pick_blocks(grad, acc, down_places(info, down_rows, *grad.shape[:2]), False)


def row_grad_kernel(n_dp, i, rows, *refs):
    lefts = refs[:n_dp]
    *rights, grad, acc, stage, sems = refs[n_dp:]
    weight_grad(acc, lefts, rights, stage, sems)
    pick_blocks(grad, acc, lambda c, k: rows[i, c, k], True)


def tokens_grad_kernel(n_dp, info, *refs):
    other_rows = refs[: n_dp - 1]
    refs = refs[n_dp - 1 :]
    sides = refs[:n_dp], refs[n_dp : 2 * n_dp]
    gate_dense, up_dense = refs[2 * n_dp : 2 * n_dp + 2]
    others = refs[2 * n_dp + 2 : 5 * n_dp - 1]
    keep, send = refs[5 * n_dp - 1 : 5 * n_dp + 1]
    scratch = refs[5 * n_dp + 1 :]
    denses = [gate_dense, *scratch[: n_dp - 1]], [up_dense, *scratch[n_dp - 1 :]]
    for n, rows in enumerate(other_rows):
        packed, mine, other = others[n :: n_dp - 1]
        scatter_rows(denses[0][n + 1], gate_pieces(packed), rows, 0)
        scatter_rows(denses[1][n + 1], half_pieces(mine, other, info[GROUP], 0), rows, 1)
    for dc in reversed(range(sides[0][0].shape[0])):
        value = 0.0
        for acts, side in zip(sides, denses):
            for act, weights in zip(acts, side):
                value += lax.dot_general(act[dc], weights[...], (((1,), (1,)), ((), ())), preferred_element_type=F32)
        put_plane(keep, send, dc, value)


def shape(dims, dtype):
    return jax.ShapeDtypeStruct(dims, dtype)


def body(n_dp, n_tok, shards, tokens, gate_blocks, up_blocks, down_blocks, gate_rows, up_rows, down_rows, cotangent):
    nj = n_dp * n_tok
    z = lax.axis_index("shard")
    x_index, c_index = lax.axis_index("dp"), lax.axis_index("tok")
    group = lax.axis_index("groups")
    assert gate_blocks.shape[0] == lax.axis_size("groups") == 2
    q = column_shard(n_dp, z, x_index, c_index)
    count, width = tokens.shape
    columns, nonzero, size, _ = gate_blocks.shape
    per_owner = nonzero // shards
    owned = width // size
    hidden_width = columns * size
    part = count // shards
    blocks = columns * per_owner

    def reduce(near, far):
        bit = 1
        while bit < shards:
            arrived = lax.ppermute(far, ("shard", "dp"), shard_perm(shards, n_dp, bit))
            if near.shape[0] == 1:
                return near, arrived
            half = (near.shape[0] // 2, *near.shape[1:])
            near, far = run(
                functools.partial(add_kernel, n_dp, n_tok, bit), [], [near, arrived], [shape(half, F32), shape(half, BF)], [], 0
            )
            bit *= 2

    def gather(own):
        have = {0: own}
        bit = shards // 2
        while bit:
            for d in sorted(have):
                have[d ^ bit] = lax.ppermute(have[d], ("shard", "dp"), shard_perm(shards, n_dp, bit))
            bit //= 2
        return [have[d] for d in range(shards)]

    def run(kernel, scalars, arrays, outs, scratch, flops, kept=(), limit=LIMIT, out_spaces=None):
        return call(kernel, scalars, arrays, outs, scratch, flops, kept, limit, out_spaces)

    def gather_plane(own):
        got = []
        for dx in range(n_dp):
            base = own if dx == 0 else lax.ppermute(own, "dp", xor_perm(n_dp, dx))
            got.append(base)
            for dc in range(1, n_tok):
                got.append(lax.ppermute(base, "tok", xor_perm(n_tok, dc)))
        return got

    w_perm = weight_perm(shards, n_dp, n_tok)
    owner = weight_owner(shards, n_dp, n_tok, z, x_index, c_index)
    info = jnp.stack([v.astype(jnp.int32) for v in (z, q, owner, jnp.int32(owned), group)])
    rows, gate_part, half_mine = run(
        pack_kernel,
        [info, gate_rows, up_rows],
        [],
        [shape((2, columns, per_owner), jnp.int32)] + [shape((n * blocks, size, size), BF) for n in (1, 1)],
        [pltpu.SemaphoreType.DMA((columns + 2,))],
        0,
        [gate_blocks, up_blocks, down_blocks],
        60 << 20,
        [pltpu.SMEM] + [pltpu.VMEM] * 2,
    )
    gate_part = lax.ppermute(gate_part, PLANE, w_perm)
    rows = lax.ppermute(rows, PLANE, w_perm)
    half_mine = lax.ppermute(half_mine, PLANE, w_perm)
    half_other = lax.ppermute(half_mine, "groups", [(0, 1), (1, 0)])

    xs = gather_plane(tokens)
    cots = gather_plane(cotangent)
    macs = nj * count * width * hidden_width * 2
    acc = pltpu.VMEM((hidden_width, width), F32)
    dense = shape((width, hidden_width), BF)

    parts = (shards // 2, nj, part, hidden_width)
    part_shapes = [shape(parts, F32), shape(parts, BF)]

    sums_scratch = [pltpu.VMEM((nj, count, hidden_width), F32)]

    def project(kernel, weights):
        return run(
            functools.partial(kernel, nj), [info, rows], [*xs, *weights], part_shapes + [dense], sums_scratch, macs
        )

    near_gate, far_gate, gate_dense = project(gate_kernel, [gate_part])
    gates = reduce(near_gate, far_gate)
    near_up, far_up, up_dense = project(up_kernel, [half_mine, half_other])
    ups = reduce(near_up, far_up)
    near_hg, far_hg, down_dense = run(
        functools.partial(hidden_grad_kernel, nj, columns),
        [info, down_rows],
        [*cots, half_mine, half_other],
        part_shapes + [shape((hidden_width, width), BF)],
        sums_scratch,
        macs,
    )
    near_hg, last_hg = reduce(near_hg, far_hg)
    act = shape((nj, part, hidden_width), BF)
    sums, hidden = run(
        hidden_kernel, [], [*gates, *ups], [shape((2, nj, part, hidden_width), F32), act], [], macs // 64
    )
    gate_act, up_act = run(act_grad_kernel, [], [sums, near_hg, last_hg], [act, act], [], macs // 64)

    chip = shape((n_tok, count, hidden_width), BF)
    others = range(1, n_dp)
    to_dp = lambda a, dx: lax.ppermute(a, "dp", xor_perm(n_dp, dx))
    other_gate = [to_dp(gate_part, dx) for dx in others]
    other_rows = [to_dp(rows, dx) for dx in others]
    other_halves = [to_dp(half, dx) for half in (half_mine, half_other) for dx in others]

    def join(own):
        parts = gather(own)
        joined = run(functools.partial(join_kernel, shards, n_dp, n_tok), [info], parts, [chip] * n_dp, [], 0)
        return joined, [joined[0]] + [to_dp(joined[dx], dx) for dx in others]

    all_hidden, chip_hidden = join(hidden)
    all_gate, chip_gate = join(gate_act)
    all_up, chip_up = join(up_act)

    plane_shapes = [shape((count, width), F32), shape((n_tok - 1, count, width), BF)]
    grad_shape = shape((columns, per_owner, size, size), BF)
    staged = [acc, pltpu.VMEM((nj, count, width), BF), pltpu.SemaphoreType.DMA((nj,))]
    mixed = run(
        functools.partial(mixed_kernel, n_dp, columns),
        [info, down_rows],
        [*chip_hidden, down_dense, *other_halves],
        plane_shapes,
        [pltpu.VMEM((hidden_width, width), BF)] * (n_dp - 1),
        macs,
    )
    (down_grad,) = run(
        functools.partial(down_grad_kernel, n_dp), [info, down_rows], all_hidden, [grad_shape], staged, macs, cots
    )

    def row_grad(i, lefts):
        kernel = functools.partial(row_grad_kernel, n_dp, i)
        return run(kernel, [rows], lefts, [grad_shape], staged, macs, xs)[0]

    gate_grad = row_grad(0, all_gate)
    up_grad = row_grad(1, all_up)
    tokens_terms = run(
        functools.partial(tokens_grad_kernel, n_dp),
        [info, *other_rows],
        [*chip_gate, *chip_up, gate_dense, up_dense, *other_gate, *other_halves],
        plane_shapes,
        [pltpu.VMEM((width, hidden_width), BF)] * (2 * n_dp - 2),
        2 * macs,
    )

    def sum_plane(terms):
        keep, send = terms
        if n_tok == 2:
            arrived = [lax.ppermute(send, "tok", xor_perm(n_tok, 1))]
        else:
            arrived = [lax.ppermute(send[dc - 1], "tok", xor_perm(n_tok, dc)) for dc in range(1, n_tok)]
        return run(sum_kernel, [], [keep, *arrived], [shape((count, width), BF)], [], 0)[0]

    g_perm = grad_perm(shards, n_dp, n_tok)

    def home(grad):
        grad = lax.ppermute(grad, PLANE, g_perm)
        return run(deliver_kernel, [], [grad], [grad_shape], [], 0)[0]

    return (sum_plane(mixed), sum_plane(tokens_terms), home(gate_grad), home(up_grad), home(down_grad))


def solution(mesh):
    shards, n_dp, n_tok = (mesh.shape[name] for name in PLANE)
    assert shards == n_dp * n_tok
    in_specs = (
        P(("groups", "dp", "tok"), "shard"),
        P("shard", None, None, None),
        P("shard", None, None, None),
        P("shard", None, None, None),
        P("shard", None),
        P("shard", None),
        P(),
        P(("groups", "dp", "tok"), "shard"),
    )
    out_specs = (
        P(("groups", "dp", "tok"), "shard"),
        P(("groups", "dp", "tok"), "shard"),
        P(("groups", "shard"), ("dp", "tok"), None, None),
        P(("groups", "shard"), ("dp", "tok"), None, None),
        P(("groups", "shard"), ("dp", "tok"), None, None),
    )
    program = functools.partial(body, n_dp, n_tok, shards)
    return jax.shard_map(program, mesh=mesh, in_specs=in_specs, out_specs=out_specs, check_vma=False)
```

```python
import functools

import jax
import jax.numpy as jnp
from jax import lax
from jax.experimental import pallas as pl
from jax.experimental.pallas import tpu as pltpu
from jax.sharding import PartitionSpec as P

BF = jnp.bfloat16
F32 = jnp.float32
LIMIT = 16 << 20
Z, Q, _, OWNED, GROUP = range(5)
PLANE = ("shard", "dp", "tok")


def xor_perm(count, step):
    return [(i, i ^ step) for i in range(count)]


def column_shard(n_dp, z, x, c):
    return c * n_dp + (x ^ (z & 1))


def shard_perm(shards, n_dp, d):
    return [(z * n_dp + x, (z ^ d) * n_dp + (x ^ (d & 1))) for z in range(shards) for x in range(n_dp)]


def weight_perm(shards, n_dp, n_tok):
    pairs = []
    for z in range(shards):
        for x in range(n_dp):
            for c in range(n_tok):
                source = x * n_tok + z // 2 if (shards, n_dp, n_tok) == (4, 2, 2) else z
                plane = column_shard(n_dp, z, x, c) * n_dp * n_tok
                pairs.append((plane + source, (z * n_dp + x) * n_tok + c))
    return pairs


def weight_owner(shards, n_dp, n_tok, z, x, c):
    if (shards, n_dp, n_tok) == (4, 2, 2):
        return c * 2 + (x ^ (z & 1))
    return x * n_tok + c


def grad_perm(shards, n_dp, n_tok):
    return [
        ((z * n_dp + x) * n_tok + c, column_shard(n_dp, z, x, c) * n_dp * n_tok + z)
        for z in range(shards)
        for x in range(n_dp)
        for c in range(n_tok)
    ]


def vmem(count):
    return [pl.BlockSpec(memory_space=pltpu.VMEM)] * count


def smem(count):
    return [pl.BlockSpec(memory_space=pltpu.SMEM)] * count


def call(kernel, scalars, arrays, outs, scratch, flops, kept, limit, out_spaces):
    moved = sum(a.size * a.dtype.itemsize for a in (*arrays, *kept))
    moved += sum(o.size * o.dtype.itemsize for o in outs)
    return pl.pallas_call(
        kernel,
        out_shape=outs,
        in_specs=smem(len(scalars)) + vmem(len(arrays)) + [pl.BlockSpec(memory_space=pltpu.HBM)] * len(kept),
        out_specs=[pl.BlockSpec(memory_space=s) for s in out_spaces] if out_spaces else vmem(len(outs)),
        scratch_shapes=scratch,
        compiler_params=pltpu.CompilerParams(vmem_limit_bytes=limit),
        cost_estimate=pl.CostEstimate(flops=flops, bytes_accessed=moved, transcendentals=0),
    )(*scalars, *arrays, *kept)


def aligned(value, size):
    return value * size if isinstance(value, int) else pl.multiple_of(value * size, size)


def down_places(info, down_rows, columns, per_owner, dx=0):
    first_row, first = (info[Q] ^ dx) * columns, info[Z] * per_owner
    return lambda c, k: down_rows[first_row + c, first + k] - info[Z] * info[OWNED]


def scatter_cols(dense, pieces, place):
    dense[...] = jnp.zeros_like(dense)
    for blocks, c in pieces:
        per_owner, size, _ = blocks.shape
        for k in range(per_owner):
            here = pl.ds(aligned(place(c, k), size), size)
            dense[pl.ds(aligned(c, size), size), here] = blocks[k]


def split_rows(total, r, near, far, z):
    rows = near.shape[2]
    for d in range(2 * near.shape[0]):
        out = far if d % 2 else near
        out[d // 2, r] = total[r, pl.ds(aligned(z ^ d, rows), rows), :].astype(out.dtype)


def pack_kernel(mesh_sizes, owned, gate_rows, up_rows, gate, up, down, rows_out, gate_out, half_out, sems):
    columns, per_owner = rows_out.shape[1:]
    owner = weight_owner(*mesh_sizes, *(lax.axis_index(name) for name in PLANE))
    group = lax.axis_index("groups")
    here = pl.ds(owner * per_owner, per_owner)
    pairs = [(gate.at[c, here], gate_out.at[pl.ds(c * per_owner, per_owner)]) for c in range(columns)]
    pairs.append((up.at[group, here], half_out.at[pl.ds(0, per_owner)]))
    pairs.append((down.at[group, here], half_out.at[pl.ds(per_owner, per_owner)]))
    copies = [pltpu.make_async_copy(source, target, sems.at[n]) for n, (source, target) in enumerate(pairs)]
    for copy in copies:
        copy.start()
    for i, rows in enumerate((gate_rows, up_rows)):
        for c in range(columns):
            for k in range(per_owner):
                rows_out[i, c, k] = rows[c, owner * per_owner + k] - owner * owned
    for copy in copies:
        copy.wait()


def gate_pieces(packed):
    per_owner = packed.shape[0] // 2
    return [(packed.at[pl.ds(c * per_owner, per_owner)], c) for c in range(2)]


def half_pieces(mine, other, group, i):
    per_owner = mine.shape[0] // 2
    here = pl.ds(i * per_owner, per_owner)
    return [(mine.at[here], group), (other.at[here], 1 - group)]


def scatter_rows(dense, pieces, rows, i):
    dense[...] = jnp.zeros_like(dense)
    for blocks, c in pieces:
        per_owner, size, _ = blocks.shape
        for k in range(per_owner):
            place = pl.ds(aligned(rows[i, c, k], size), size)
            dense[place, pl.ds(aligned(c, size), size)] = blocks[k]


def gate_kernel(n, info, rows, *refs):
    xs, packed = refs[:n], refs[n]
    near, far, dense, total = refs[n + 1 :]
    scatter_rows(dense, gate_pieces(packed), rows, 0)
    project(xs, near, far, dense, total, info[Z])


def up_kernel(n, info, rows, *refs):
    xs, (mine, other) = refs[:n], refs[n : n + 2]
    near, far, dense, total = refs[n + 2 :]
    scatter_rows(dense, half_pieces(mine, other, info[GROUP], 0), rows, 1)
    project(xs, near, far, dense, total, info[Z])


def project(xs, near, far, dense, total, z):
    for r, x in enumerate(xs):
        total[r] = jnp.dot(x[...], dense[...], preferred_element_type=F32)
        split_rows(total, r, near, far, z)


def hidden_grad_kernel(nj, columns, info, down_rows, *refs):
    cots, (mine, other) = refs[:nj], refs[nj : nj + 2]
    near, far, down_dense, total = refs[nj + 2 :]
    place = down_places(info, down_rows, columns, mine.shape[0] // 2)
    scatter_cols(down_dense, half_pieces(mine, other, info[GROUP], 1), place)
    for r in range(nj):
        total[r] = lax.dot_general(
            cots[r][...], down_dense[...], (((1,), (1,)), ((), ())), preferred_element_type=F32
        )
        split_rows(total, r, near, far, info[Z])


def own_place(dx, d):
    return dx ^ (d & 1)


def add_kernel(n_dp, n_tok, bit, near, arrived, near_out, far_out):
    for d in range(near.shape[0]):
        out = far_out if d % 2 else near_out
        for dx in range(n_dp):
            there = pl.ds(own_place(dx, bit) * n_tok, n_tok)
            here = pl.ds(dx * n_tok, n_tok)
            out[d // 2, here] = (near[d, here] + arrived[d, there].astype(F32)).astype(out.dtype)


def hidden_kernel(gate_near, gate_last, up_near, up_last, sums, hidden):
    gate = gate_near[0] + gate_last[0].astype(F32)
    up = up_near[0] + up_last[0].astype(F32)
    sums[0] = gate
    sums[1] = up
    hidden[...] = (gate * jax.nn.sigmoid(gate) * up).astype(BF)


def act_grad_kernel(sums, near, last, gate_act, up_act):
    hidden_grad = near[0] + last[0].astype(F32)
    gate, up = sums[0], sums[1]
    s = jax.nn.sigmoid(gate)
    gate_act[...] = (hidden_grad * up * s * (1.0 + gate * (1.0 - s))).astype(BF)
    up_act[...] = (hidden_grad * (gate * s)).astype(BF)


def join_kernel(shards, n_dp, n_tok, info, *refs):
    parts, joined = refs[:shards], refs[shards:]
    rows = parts[0].shape[1]
    for dx in range(n_dp):
        for dc in range(n_tok):
            for d, part in enumerate(parts):
                here = pl.ds(aligned(info[Z] ^ d, rows), rows)
                joined[dx][dc, here, :] = part[own_place(dx, d) * n_tok + dc]


def weight_grad(acc, lefts, rights, stage, sems):
    copies = [pltpu.make_async_copy(right, stage.at[r], sems.at[r]) for r, right in enumerate(rights)]
    for copy in copies:
        copy.start()
    n_tok = lefts[0].shape[0]
    for r, copy in enumerate(copies):
        copy.wait()
        left = lefts[r // n_tok][r % n_tok]
        term = lax.dot_general(left, stage[r], (((0,), (0,)), ((), ())), preferred_element_type=F32)
        if r == 0:
            acc[...] = term
        else:
            acc[...] += term


def pick_blocks(out, acc, place, transposed):
    columns, per_owner, size, _ = out.shape
    for c in range(columns):
        for k in range(per_owner):
            block = acc[c * size : (c + 1) * size, pl.ds(aligned(place(c, k), size), size)]
            out[c, k] = (block.T if transposed else block).astype(BF)


def sum_kernel(first, *refs):
    *others, out = refs
    total = first[...]
    for other in others:
        value = other[...].astype(F32)
        total += value if value.ndim == total.ndim else jnp.sum(value, axis=0)
    out[...] = total.astype(BF)


def deliver_kernel(*refs):
    count = len(refs) // 2
    for source, out in zip(refs[:count], refs[count:]):
        out[...] = source[...]


def put_plane(keep, send, dc, value):
    if dc == 0:
        keep[...] = value
    else:
        send[dc - 1] = value.astype(BF)


def mixed_kernel(n_dp, columns, info, down_rows, *refs):
    hiddens, dense = refs[:n_dp], refs[n_dp]
    halves = refs[n_dp + 1 : 3 * n_dp - 1]
    keep, send = refs[3 * n_dp - 1 : 3 * n_dp + 1]
    denses = [dense, *refs[3 * n_dp + 1 :]]
    for dx in range(1, n_dp):
        mine, other = halves[dx - 1], halves[n_dp + dx - 2]
        place = down_places(info, down_rows, columns, mine.shape[0] // 2, dx)
        scatter_cols(denses[dx], half_pieces(mine, other, info[GROUP], 1), place)
    for dc in reversed(range(hiddens[0].shape[0])):
        value = 0.0
        for hidden, weights in zip(hiddens, denses):
            value += jnp.dot(hidden[dc], weights[...], preferred_element_type=F32)
        put_plane(keep, send, dc, value)


def down_grad_kernel(n_dp, info, down_rows, *refs):
    lefts = refs[:n_dp]
    *rights, grad, acc, stage, sems = refs[n_dp:]
    weight_grad(acc, lefts, rights, stage, sems)
    pick_blocks(grad, acc, down_places(info, down_rows, *grad.shape[:2]), False)


def row_grad_kernel(n_dp, i, rows, *refs):
    lefts = refs[:n_dp]
    *rights, grad, acc, stage, sems = refs[n_dp:]
    weight_grad(acc, lefts, rights, stage, sems)
    pick_blocks(grad, acc, lambda c, k: rows[i, c, k], True)


def tokens_grad_kernel(n_dp, info, *refs):
    other_rows = refs[: n_dp - 1]
    refs = refs[n_dp - 1 :]
    sides = refs[:n_dp], refs[n_dp : 2 * n_dp]
    gate_dense, up_dense = refs[2 * n_dp : 2 * n_dp + 2]
    others = refs[2 * n_dp + 2 : 5 * n_dp - 1]
    keep, send = refs[5 * n_dp - 1 : 5 * n_dp + 1]
    scratch = refs[5 * n_dp + 1 :]
    denses = [gate_dense, *scratch[: n_dp - 1]], [up_dense, *scratch[n_dp - 1 :]]
    for n, rows in enumerate(other_rows):
        packed, mine, other = others[n :: n_dp - 1]
        scatter_rows(denses[0][n + 1], gate_pieces(packed), rows, 0)
        scatter_rows(denses[1][n + 1], half_pieces(mine, other, info[GROUP], 0), rows, 1)
    for dc in reversed(range(sides[0][0].shape[0])):
        value = 0.0
        for acts, side in zip(sides, denses):
            for act, weights in zip(acts, side):
                value += lax.dot_general(act[dc], weights[...], (((1,), (1,)), ((), ())), preferred_element_type=F32)
        put_plane(keep, send, dc, value)


def shape(dims, dtype):
    return jax.ShapeDtypeStruct(dims, dtype)


def body(n_dp, n_tok, shards, tokens, gate_blocks, up_blocks, down_blocks, gate_rows, up_rows, down_rows, cotangent):
    nj = n_dp * n_tok
    z = lax.axis_index("shard")
    x_index, c_index = lax.axis_index("dp"), lax.axis_index("tok")
    group = lax.axis_index("groups")
    assert gate_blocks.shape[0] == lax.axis_size("groups") == 2
    q = column_shard(n_dp, z, x_index, c_index)
    count, width = tokens.shape
    columns, nonzero, size, _ = gate_blocks.shape
    per_owner = nonzero // shards
    owned = width // size
    hidden_width = columns * size
    part = count // shards
    blocks = columns * per_owner

    def reduce(near, far):
        bit = 1
        while bit < shards:
            arrived = lax.ppermute(far, ("shard", "dp"), shard_perm(shards, n_dp, bit))
            if near.shape[0] == 1:
                return near, arrived
            half = (near.shape[0] // 2, *near.shape[1:])
            near, far = run(
                functools.partial(add_kernel, n_dp, n_tok, bit), [], [near, arrived], [shape(half, F32), shape(half, BF)], [], 0
            )
            bit *= 2

    def gather(own):
        have = {0: own}
        bit = shards // 2
        while bit:
            for d in sorted(have):
                have[d ^ bit] = lax.ppermute(have[d], ("shard", "dp"), shard_perm(shards, n_dp, bit))
            bit //= 2
        return [have[d] for d in range(shards)]

    def run(kernel, scalars, arrays, outs, scratch, flops, kept=(), limit=LIMIT, out_spaces=None):
        return call(kernel, scalars, arrays, outs, scratch, flops, kept, limit, out_spaces)

    def gather_plane(own):
        got = []
        for dx in range(n_dp):
            base = own if dx == 0 else lax.ppermute(own, "dp", xor_perm(n_dp, dx))
            got.append(base)
            for dc in range(1, n_tok):
                got.append(lax.ppermute(base, "tok", xor_perm(n_tok, dc)))
        return got

    w_perm = weight_perm(shards, n_dp, n_tok)
    owner = weight_owner(shards, n_dp, n_tok, z, x_index, c_index)
    info = jnp.stack([v.astype(jnp.int32) for v in (z, q, owner, jnp.int32(owned), group)])
    rows, gate_part, half_mine = run(
        functools.partial(pack_kernel, (shards, n_dp, n_tok), owned),
        [gate_rows, up_rows],
        [],
        [shape((2, columns, per_owner), jnp.int32)] + [shape((n * blocks, size, size), BF) for n in (1, 1)],
        [pltpu.SemaphoreType.DMA((columns + 2,))],
        0,
        [gate_blocks, up_blocks, down_blocks],
        60 << 20,
        [pltpu.SMEM] + [pltpu.VMEM] * 2,
    )
    gate_part = lax.ppermute(gate_part, PLANE, w_perm)
    rows = lax.ppermute(rows, PLANE, w_perm)
    half_mine = lax.ppermute(half_mine, PLANE, w_perm)
    half_other = lax.ppermute(half_mine, "groups", [(0, 1), (1, 0)])

    xs = gather_plane(tokens)
    cots = gather_plane(cotangent)
    macs = nj * count * width * hidden_width * 2
    acc = pltpu.VMEM((hidden_width, width), F32)
    dense = shape((width, hidden_width), BF)

    parts = (shards // 2, nj, part, hidden_width)
    part_shapes = [shape(parts, F32), shape(parts, BF)]

    sums_scratch = [pltpu.VMEM((nj, count, hidden_width), F32)]

    def project(kernel, weights):
        return run(
            functools.partial(kernel, nj), [info, rows], [*xs, *weights], part_shapes + [dense], sums_scratch, macs
        )

    near_gate, far_gate, gate_dense = project(gate_kernel, [gate_part])
    gates = reduce(near_gate, far_gate)
    near_up, far_up, up_dense = project(up_kernel, [half_mine, half_other])
    ups = reduce(near_up, far_up)
    near_hg, far_hg, down_dense = run(
        functools.partial(hidden_grad_kernel, nj, columns),
        [info, down_rows],
        [*cots, half_mine, half_other],
        part_shapes + [shape((hidden_width, width), BF)],
        sums_scratch,
        macs,
    )
    near_hg, last_hg = reduce(near_hg, far_hg)
    act = shape((nj, part, hidden_width), BF)
    sums, hidden = run(
        hidden_kernel, [], [*gates, *ups], [shape((2, nj, part, hidden_width), F32), act], [], macs // 64
    )
    gate_act, up_act = run(act_grad_kernel, [], [sums, near_hg, last_hg], [act, act], [], macs // 64)

    chip = shape((n_tok, count, hidden_width), BF)
    others = range(1, n_dp)
    to_dp = lambda a, dx: lax.ppermute(a, "dp", xor_perm(n_dp, dx))
    other_gate = [to_dp(gate_part, dx) for dx in others]
    other_rows = [to_dp(rows, dx) for dx in others]
    other_halves = [to_dp(half, dx) for half in (half_mine, half_other) for dx in others]

    def join(own):
        parts = gather(own)
        joined = run(functools.partial(join_kernel, shards, n_dp, n_tok), [info], parts, [chip] * n_dp, [], 0)
        return joined, [joined[0]] + [to_dp(joined[dx], dx) for dx in others]

    all_hidden, chip_hidden = join(hidden)
    all_gate, chip_gate = join(gate_act)
    all_up, chip_up = join(up_act)

    plane_shapes = [shape((count, width), F32), shape((n_tok - 1, count, width), BF)]
    grad_shape = shape((columns, per_owner, size, size), BF)
    staged = [acc, pltpu.VMEM((nj, count, width), BF), pltpu.SemaphoreType.DMA((nj,))]
    mixed = run(
        functools.partial(mixed_kernel, n_dp, columns),
        [info, down_rows],
        [*chip_hidden, down_dense, *other_halves],
        plane_shapes,
        [pltpu.VMEM((hidden_width, width), BF)] * (n_dp - 1),
        macs,
    )
    (down_grad,) = run(
        functools.partial(down_grad_kernel, n_dp), [info, down_rows], all_hidden, [grad_shape], staged, macs, cots
    )

    def row_grad(i, lefts):
        kernel = functools.partial(row_grad_kernel, n_dp, i)
        return run(kernel, [rows], lefts, [grad_shape], staged, macs, xs)[0]

    gate_grad = row_grad(0, all_gate)
    up_grad = row_grad(1, all_up)
    tokens_terms = run(
        functools.partial(tokens_grad_kernel, n_dp),
        [info, *other_rows],
        [*chip_gate, *chip_up, gate_dense, up_dense, *other_gate, *other_halves],
        plane_shapes,
        [pltpu.VMEM((width, hidden_width), BF)] * (2 * n_dp - 2),
        2 * macs,
    )

    def sum_plane(terms):
        keep, send = terms
        if n_tok == 2:
            arrived = [lax.ppermute(send, "tok", xor_perm(n_tok, 1))]
        else:
            arrived = [lax.ppermute(send[dc - 1], "tok", xor_perm(n_tok, dc)) for dc in range(1, n_tok)]
        return run(sum_kernel, [], [keep, *arrived], [shape((count, width), BF)], [], 0)[0]

    g_perm = grad_perm(shards, n_dp, n_tok)

    def home(grad):
        grad = lax.ppermute(grad, PLANE, g_perm)
        return run(deliver_kernel, [], [grad], [grad_shape], [], 0)[0]

    return (sum_plane(mixed), sum_plane(tokens_terms), home(gate_grad), home(up_grad), home(down_grad))


def solution(mesh):
    shards, n_dp, n_tok = (mesh.shape[name] for name in PLANE)
    assert shards == n_dp * n_tok
    in_specs = (
        P(("groups", "dp", "tok"), "shard"),
        P("shard", None, None, None),
        P("shard", None, None, None),
        P("shard", None, None, None),
        P("shard", None),
        P("shard", None),
        P(),
        P(("groups", "dp", "tok"), "shard"),
    )
    out_specs = (
        P(("groups", "dp", "tok"), "shard"),
        P(("groups", "dp", "tok"), "shard"),
        P(("groups", "shard"), ("dp", "tok"), None, None),
        P(("groups", "shard"), ("dp", "tok"), None, None),
        P(("groups", "shard"), ("dp", "tok"), None, None),
    )
    program = functools.partial(body, n_dp, n_tok, shards)
    return jax.shard_map(program, mesh=mesh, in_specs=in_specs, out_specs=out_specs, check_vma=False)
```
